32 devices in a mesh: dp: 4 (over y, x), space: 8 (over z, core).
Axes of the slice: x: 2, y: 2, z: 4, core: 2. Of those that a mesh axis runs over, the one named last changes fastest.
Arguments:
- volumes: bfloat16 [4, 4, 64, 32, 512], P('dp', None, 'space'), may hold values from -6 to 6
- first_kernel: bfloat16 [3, 3, 3, 4, 32], replicated, may hold values from -0.625 to 0.625
- second_kernel: float32 [3, 3, 3, 32, 64], replicated, may hold values from -0.21875 to 0.21875
- cotangent: bfloat16 [4, 64, 16, 8, 128], P('dp', None, 'space'), may hold values from -0.5 to 0.5
- first_moment: float32 [55296], P(('dp', 'space')), may hold values from -0.75 to 0.75
- second_moment: float32 [55296], P(('dp', 'space')), may hold values from 0.001 to 0.01
Outputs:
- activations: bfloat16 [4, 64, 16, 8, 128], P('dp', None, 'space')
- first_gradient: float32 [3, 3, 3, 4, 32], replicated
- new_kernel: float32 [3, 3, 3, 32, 64], replicated
- new_first_moment: float32 [55296], P(('dp', 'space'))
- new_second_moment: float32 [55296], P(('dp', 'space'))
The draws below stay inside these ranges and needn't reach their ends.
All inputs are finite; a program needn't handle non-finite values.
Results may differ from the reference program's by a relative error of at most 0.0055.
The reference program's roundings to bfloat16 on the way (of `hidden`, `kernel_half`, `delta_two` and `delta_one`) count: a program that leaves them out, or rounds other values in their place, can miss the bound.
Values may be sent and summed in bfloat16 or wider, within the bound.
No kernel may reach another device: no remote copies, remote signals or barrier semaphores. Data moves between devices by JAX's collectives and lax.ppermute only.
A program may use at most 256 MiB of HBM per device.

```python
import math
import jax
import jax.numpy as jnp
from jax import lax

CIN = 4
C1 = 32
C2 = 64
Y = 32
X = 512
VOLS = 4
Z = 64
FLAT = 55296


def level_of(rng, extent, shards, low, high):
    level = 1.0
    for position, shards_of in shards:
        steps = jax.random.uniform(jax.random.fold_in(jax.random.fold_in(rng, 6), position), (shards_of,), jnp.float32, low / len(shards), high / len(shards))
        level = level * jnp.repeat(jnp.exp(steps), extent[position] // shards_of).reshape((-1,) + (1,) * (len(extent) - 1 - position))
    return level


def bell_draw(key, extent, width, reach, shards=(), dtype=jnp.bfloat16):
    result = width * jax.random.normal(key, extent, jnp.float32)
    if shards:
        result = result * level_of(key, extent, shards, -0.22, 0.18)
    return jnp.clip(result, -reach, reach).astype(dtype)


def setup_inputs(seed: int = 0) -> dict:
    keys = jax.random.split(jax.random.key(seed), 7)
    return {
        "volumes": bell_draw(keys[0], (VOLS, CIN, Z, Y, X), 1.0, 6.0, ((0, 4), (2, 8))),
        "first_kernel": bell_draw(keys[1], (3, 3, 3, CIN, C1), (27 * CIN) ** -0.5, 0.625),
        "second_kernel": bell_draw(keys[2], (3, 3, 3, C1, C2), (27 * C1) ** -0.5, 0.21875, (), jnp.float32),
        "cotangent": bell_draw(keys[3], (VOLS, C2, Z // 4, Y // 4, X // 4), (8.0 / (VOLS * Z * Y * X // 64) ** 0.5), 0.5, ((0, 4), (2, 8))),
        "first_moment": bell_draw(keys[4], (FLAT,), 0.05, 0.75, ((0, 32),), jnp.float32),
        "second_moment": jnp.clip(jnp.exp(math.log(0.01) - 2.30258502 * jax.random.uniform(keys[5], (FLAT,), jnp.float32) ** level_of(keys[5], (FLAT,), ((0, 32),), -0.2, 0.2)), 0.001, 0.01),
    }


SLOPE = 0.3
BETA_FIRST = 0.9
BETA_SECOND = 0.999
LEARN_RATE = 0.001
EPSILON = 1e-08
NUMBERS = ('NCDHW', 'DHWIO', 'NCDHW')

def strided(inputs, kernel):
    return lax.conv_general_dilated(inputs, kernel, (2, 2, 2), [(1, 1), (1, 1), (1, 1)], dimension_numbers=NUMBERS, preferred_element_type=jnp.float32)

def strided_exact(inputs, kernel):
    return lax.conv_general_dilated(inputs, kernel, (2, 2, 2), [(1, 1), (1, 1), (1, 1)], dimension_numbers=NUMBERS, preferred_element_type=jnp.float32)

def leaky(values):
    return jnp.where(values > 0, values, SLOPE * values)

def leaky_slope(values):
    return jnp.where(values > 0, jnp.float32(1.0), jnp.float32(SLOPE))

def reference(volumes, first_kernel, second_kernel, cotangent, first_moment, second_moment):
    kernel_half = second_kernel.astype(jnp.bfloat16)
    first_wide = first_kernel.astype(jnp.float32)
    second_wide = kernel_half.astype(jnp.float32)

    def one_volume(carry, pair):
        sum_first, sum_second = carry
        volume, cotan = pair
        inputs = volume[None]
        preact_one = strided(inputs, first_kernel)
        hidden = leaky(preact_one).astype(jnp.bfloat16)
        preact_two = strided(hidden, kernel_half)
        output = leaky(preact_two).astype(jnp.bfloat16)
        delta_two = (cotan[None].astype(jnp.float32) * leaky_slope(preact_two)).astype(jnp.bfloat16)

        def second_map(activ, kernel):
            return strided_exact(activ, kernel)
        _, pull_second = jax.vjp(second_map, hidden.astype(jnp.float32), second_wide)
        grad_hidden, grad_second = pull_second(delta_two.astype(jnp.float32))
        delta_one = (grad_hidden * leaky_slope(preact_one)).astype(jnp.bfloat16)
        wide_inputs = inputs.astype(jnp.float32)

        def first_map(kernel):
            return strided_exact(wide_inputs, kernel)
        _, pull_first = jax.vjp(first_map, first_wide)
        grad_first, = pull_first(delta_one.astype(jnp.float32))
        return ((sum_first + grad_first, sum_second + grad_second), output[0])
    start = (jnp.zeros(first_kernel.shape, jnp.float32), jnp.zeros(second_kernel.shape, jnp.float32))
    (first_gradient, second_gradient), activations = lax.scan(one_volume, start, (volumes, cotangent))
    flat_grad = second_gradient.reshape(-1)
    new_first = BETA_FIRST * first_moment + (1.0 - BETA_FIRST) * flat_grad
    new_second = BETA_SECOND * second_moment + (1.0 - BETA_SECOND) * flat_grad * flat_grad
    step_size = LEARN_RATE * new_first / (jnp.sqrt(new_second) + EPSILON)
    new_kernel = second_kernel - step_size.reshape(second_kernel.shape)
    return (activations, first_gradient, new_kernel, new_first, new_second)
```

```python
import jax
import jax.numpy as jnp
import numpy as np
from jax import lax
from jax.experimental import pallas as pl
from jax.experimental.pallas import tpu as pltpu
from jax.sharding import PartitionSpec as P

SLOPE = 0.3
BETA_FIRST = 0.9
BETA_SECOND = 0.999
LEARN_RATE = 0.001
EPSILON = 1e-08
BF = jnp.bfloat16
F32 = jnp.float32
AXES = ("dp", "space")
LANES = 128


def along(value, axis, steps):
    count = lax.axis_size(axis)
    first, last = (max(0, -steps), min(count, count - steps))
    return lax.ppermute(value, axis, [(source, source + steps) for source in range(first, last)])


def leaky(values):
    return jnp.where(values > 0, values, SLOPE * values)


def nn(a, b):
    return lax.dot_general(a, b, (((1,), (0,)), ((), ())), preferred_element_type=F32)


def nt(a, b):
    return lax.dot_general(a, b, (((1,), (1,)), ((), ())), preferred_element_type=F32)


def tn(a, b):
    return lax.dot_general(a, b, (((0,), (0,)), ((), ())), preferred_element_type=F32)


def spread_taps():
    table = np.zeros((3, 3, 4, 2, 2, 256), np.float32)
    for dy in range(3):
        for dx in range(3):
            for c in range(4):
                for row in range(2):
                    for p in range(2):
                        table[dy, dx, c, row, p, (2 * row + dy) * 32 + (2 * p + dx) * 4 + c] = 1
    return table.reshape(36, 1024)


def forward_kernel(v_ref, vh_ref, w1_ref, e_ref, w2_ref, cot_ref,
                   act_ref, d_ref, h_ref, d2_ref, edge_ref,
                   sel, stage, t1, rows_c, rows_a):
    lane = lax.broadcasted_iota(jnp.int32, (512, LANES), 1)
    row = lax.broadcasted_iota(jnp.int32, (512, LANES), 0)
    base = row - 4 * lane
    for r in range(5):
        sel[:, r * LANES:(r + 1) * LANES] = jnp.where(base == r - 1, 1.0, 0.0).astype(BF)
    for dz in range(3):
        taps = tn(w1_ref[dz], e_ref[...]).astype(BF)
        for b in range(4):
            t1[dz, b * 32:(b + 1) * 32, :] = taps[:, b * 256:b * 256 + 160]
    stage[...] = jnp.zeros_like(stage)
    lane32 = lax.broadcasted_iota(jnp.int32, (32, LANES), 1)

    def plane(source, z, out):
        x = source[:, z].reshape(128, 512)
        parts = nn(x, sel[...])
        for r in range(5):
            for c in range(4):
                stage[pl.ds(32 + r * 4 + c, 32, stride=32), :] = parts[c * 32:(c + 1) * 32, r * LANES:(r + 1) * LANES]
        d_ref[out] = stage[...].astype(BF)

    @pl.loop(0, 3)
    def _(z):
        plane(vh_ref, z, z)

    @pl.loop(0, 8)
    def _(z):
        plane(v_ref, z, z + 3)

    @pl.loop(0, 5)
    def _(z):
        h_ref[z, 0:96] = jnp.zeros((96, LANES), BF)
        for m in range(8):
            acc = nn(t1[0], d_ref[2 * z, m * 128:m * 128 + 160])
            acc += nn(t1[1], d_ref[2 * z + 1, m * 128:m * 128 + 160])
            acc += nn(t1[2], d_ref[2 * z + 2, m * 128:m * 128 + 160])
            hid = leaky(acc)
            for i in range(2):
                at = (2 * m + i + 1) * 96
                odd = hid[i * 64 + 32:i * 64 + 64]
                h_ref[z, at:at + 32] = jnp.where(lane32 == 0, 0.0, pltpu.roll(odd, 1, 1)).astype(BF)
                h_ref[z, at + 32:at + 96] = hid[i * 64:i * 64 + 64].astype(BF)

    lane64 = lax.broadcasted_iota(jnp.int32, (64, LANES), 1)
    for z in range(2):
        rows_c[...] = cot_ref[:, z].astype(F32).reshape(512, LANES)
        d2_ref[z, 1024:1152] = jnp.zeros((128, LANES), BF)
        for y in range(8):
            acc = nn(w2_ref[0], h_ref[2 * z, y * 192:y * 192 + 288])
            acc += nn(w2_ref[1], h_ref[2 * z + 1, y * 192:y * 192 + 288])
            acc += nn(w2_ref[2], h_ref[2 * z + 2, y * 192:y * 192 + 288])
            rows_a[pl.ds(y, 64, stride=8), :] = leaky(acc)
            cot = rows_c[pl.ds(y, 64, stride=8), :]
            delta = cot * jnp.where(acc > 0, 1.0, SLOPE)
            low = delta.astype(BF)
            d2_ref[z, y * 128:y * 128 + 64] = low
            if z == 0:
                edge_ref[y * 64:y * 64 + 64] = low
            left = jnp.where(lane64 == LANES - 1, 0.0, pltpu.roll(delta, LANES - 1, 1))
            d2_ref[z, y * 128 + 64:y * 128 + 128] = left.astype(BF)
        act_ref[:, z] = rows_a[...].astype(BF).reshape(64, 8, LANES)


def backward_kernel(d_ref, h_ref, d2_ref, above_ref, l_ref, g2_ref, g1_ref, d2h, d1):
    lane64 = lax.broadcasted_iota(jnp.int32, (64, LANES), 1)
    d2h[1024:1152] = jnp.zeros((128, LANES), BF)
    for y in range(8):
        low = above_ref[y * 64:y * 64 + 64]
        left = jnp.where(lane64 == LANES - 1, 0.0, pltpu.roll(low.astype(F32), LANES - 1, 1))
        d2h[y * 128:y * 128 + 64] = low
        d2h[y * 128 + 64:y * 128 + 128] = left.astype(BF)

    for dz in range(3):
        acc = jnp.zeros((288, 64), F32)
        for y in range(8):
            a = jnp.concatenate([h_ref[dz, y * 192:y * 192 + 288], h_ref[dz + 2, y * 192:y * 192 + 288]], axis=1)
            b = jnp.concatenate([d2_ref[0, y * 128:y * 128 + 64], d2_ref[1, y * 128:y * 128 + 64]], axis=1)
            acc += nt(a, b)
        g2_ref[dz] = acc

    def slope(z, m):
        parts = [jnp.where(h_ref[z + 1, (2 * m + i + 1) * 96 + 32:(2 * m + i + 1) * 96 + 96].astype(F32) > 0, 1.0, SLOPE) for i in range(2)]
        return jnp.concatenate(parts, axis=0)

    for m in range(8):
        r0 = nn(l_ref[128:384], d2_ref[0, m * 128:m * 128 + 256])
        r1 = nn(l_ref[...], d2_ref[1, m * 128:m * 128 + 256])
        r2 = nn(l_ref[0:128], d2h[m * 128:m * 128 + 256])
        grads = (r0[0:128], r0[128:256] + r1[0:128], r1[128:256], r1[256:384] + r2)
        for z in range(4):
            d1[z, m * 128:m * 128 + 128] = (grads[z] * slope(z, m)).astype(BF)

    for dz in range(3):
        acc = jnp.zeros((160, LANES), F32)
        for m in range(8):
            for zz in range(2):
                z = 2 * zz
                a = jnp.concatenate([d_ref[2 * z + 2 + dz, m * 128:m * 128 + 160], d_ref[2 * z + 4 + dz, m * 128:m * 128 + 160]], axis=1)
                b = jnp.concatenate([d1[z, m * 128:m * 128 + 128], d1[z + 1, m * 128:m * 128 + 128]], axis=1)
                acc += nt(a, b)
        for dy in range(3):
            total = jnp.zeros((16, LANES), F32)
            for i in range(2):
                for p in range(2):
                    at = (2 * i + dy) * 32 + 8 * p
                    block = acc[at:at + 16]
                    shift = (2 * i + p) * 32
                    total += block if shift == 0 else pltpu.roll(block, LANES - shift, 1)
            g1_ref[dz * 3 + dy] = total[0:12, 0:32]


VMEM = pl.BlockSpec(memory_space=pltpu.VMEM)


def call(kernel, outs, scratch, args):
    return pl.pallas_call(
        kernel,
        out_shape=[jax.ShapeDtypeStruct(s, t) for s, t in outs],
        in_specs=[VMEM] * len(args),
        out_specs=[VMEM] * len(outs),
        scratch_shapes=scratch,
        compiler_params=pltpu.CompilerParams(vmem_limit_bytes=56 * 1024 * 1024),
    )(*args)


def scatter_sum(values):
    return lax.all_to_all(values, AXES, 0, 0, tiled=True).sum(0)


def gather(values, count):
    wide = jnp.broadcast_to(values[None], (count,) + values.shape)
    return lax.all_to_all(wide, AXES, 0, 0, tiled=True)


def shards(volumes, first_kernel, second_kernel, cotangent, first_moment, second_moment):
    count = lax.axis_size(AXES)
    below = along(volumes[0, :, -3:], "space", 1)
    kernel_half = second_kernel.astype(BF)
    w2 = kernel_half.reshape(3, 288, 64).transpose(0, 2, 1)
    zero = jnp.zeros((3, 32, 64), BF)
    tap = lambda dy, dx: kernel_half[:, dy, dx]
    lines = (
        (tap(1, 1), zero, zero, zero),
        (tap(1, 2), tap(1, 0), zero, zero),
        (tap(2, 1), zero, tap(0, 1), zero),
        (tap(2, 2), tap(2, 0), tap(0, 2), tap(0, 0)),
    )
    back = jnp.concatenate([jnp.concatenate(line, axis=2) for line in lines], axis=1).reshape(384, 256)
    act, d, h, d2, edge = call(
        forward_kernel,
        [((64, 2, 8, LANES), BF), ((11, 1056, LANES), BF), ((5, 1632, LANES), BF), ((2, 1152, LANES), BF), ((512, LANES), BF)],
        [pltpu.VMEM((512, 640), BF), pltpu.VMEM((1056, LANES), F32), pltpu.VMEM((3, 128, 160), BF),
         pltpu.VMEM((512, LANES), F32), pltpu.VMEM((512, LANES), F32)],
        (volumes[0], below, first_kernel.reshape(3, 36, 32), jnp.asarray(spread_taps(), BF), w2, cotangent[0]),
    )
    above = along(edge, "space", -1)
    g2, g1 = call(
        backward_kernel,
        [((3, 288, 64), F32), ((9, 12, 32), F32)],
        [pltpu.VMEM((1152, LANES), BF), pltpu.VMEM((4, 1024, LANES), BF)],
        (d, h, d2, above, back),
    )
    share = first_moment.shape[0]
    one = g1.reshape(-1)
    pad = -one.shape[0] % count
    one = jnp.pad(one, (0, pad)).reshape(count, -1)
    both = scatter_sum(jnp.concatenate([g2.reshape(count, share), one], axis=1))
    grad_share = both[:share]
    offset = lax.axis_index(AXES) * share
    new_first = BETA_FIRST * first_moment + (1.0 - BETA_FIRST) * grad_share
    new_second = BETA_SECOND * second_moment + (1.0 - BETA_SECOND) * grad_share * grad_share
    kernel_share = lax.dynamic_slice_in_dim(second_kernel.reshape(-1), offset, share, 0)
    updated = kernel_share - LEARN_RATE * new_first / (jnp.sqrt(new_second) + EPSILON)
    full = gather(jnp.concatenate([updated, both[share:]]), count)
    new_kernel = full[:, :share].reshape(second_kernel.shape)
    first_gradient = full[:, share:].reshape(-1)[:first_kernel.size].reshape(first_kernel.shape)
    return (act[None], first_gradient, new_kernel, new_first, new_second)


def solution(mesh):
    field = P("dp", None, "space", None, None)
    flat = P(AXES)
    return jax.shard_map(
        shards, mesh=mesh, in_specs=(field, P(), P(), field, flat, flat),
        out_specs=(field, P(), P(), flat, flat), check_vma=False)
```

```python
import functools
import jax
import jax.numpy as jnp
import numpy as np
from jax import lax
from jax.experimental import pallas as pl
from jax.experimental.pallas import tpu as pltpu
from jax.sharding import PartitionSpec as P

SLOPE = 0.3
BETA_FIRST = 0.9
BETA_SECOND = 0.999
LEARN_RATE = 0.001
EPSILON = 1e-08
BF = jnp.bfloat16
F32 = jnp.float32
AXES = ("dp", "space")
LANES = 128


def along(value, axis, steps):
    count = lax.axis_size(axis)
    first, last = (max(0, -steps), min(count, count - steps))
    return lax.ppermute(value, axis, [(source, source + steps) for source in range(first, last)])


def leaky(values):
    return jnp.where(values > 0, values, SLOPE * values)


def nn(a, b):
    return lax.dot_general(a, b, (((1,), (0,)), ((), ())), preferred_element_type=F32)


def nt(a, b):
    return lax.dot_general(a, b, (((1,), (1,)), ((), ())), preferred_element_type=F32)


def tn(a, b):
    return lax.dot_general(a, b, (((0,), (0,)), ((), ())), preferred_element_type=F32)


def spread_taps():
    table = np.zeros((3, 3, 4, 2, 2, 256), np.float32)
    for dy in range(3):
        for dx in range(3):
            for c in range(4):
                for row in range(2):
                    for p in range(2):
                        table[dy, dx, c, row, p, (2 * row + dy) * 32 + (2 * p + dx) * 4 + c] = 1
    return table.reshape(36, 1024)


def repack(source, first, count, sel, stage, out, to):
    x = jnp.concatenate([source[:, first + i].reshape(4 * 32, 512) for i in range(count)], axis=0)
    lane = lax.broadcasted_iota(jnp.int32, (32, LANES), 1)
    for r in range(4):
        part = nn(x, sel[:, r * LANES:(r + 1) * LANES])
        for i in range(count):
            for c in range(4):
                block = part[i * 128 + c * 32:i * 128 + c * 32 + 32]
                stage[i, pl.ds(32 + (r + 1) * 4 + c, 32, stride=32), :] = block
                if r == 3:
                    moved = jnp.where(lane == 0, 0.0, pltpu.roll(block, 1, 1))
                    stage[i, pl.ds(32 + c, 32, stride=32), :] = moved
    for i in range(count):
        out[to + i] = stage[i].astype(BF)


def first_section(t1, planes, outs):
    lane = lax.broadcasted_iota(jnp.int32, (32, LANES), 1)
    for ref, z in outs:
        ref[z, 0:96] = jnp.zeros((96, LANES), BF)
    for m in range(8):
        acc = nn(t1[0], planes[0](m))
        acc += nn(t1[1], planes[1](m))
        acc += nn(t1[2], planes[2](m))
        both = leaky(acc)
        for k, (ref, z) in enumerate(outs):
            hid = both[:, k * LANES:(k + 1) * LANES]
            for i in range(2):
                at = (2 * m + i + 1) * 96
                odd = hid[i * 64 + 32:i * 64 + 64]
                ref[z, at:at + 32] = jnp.where(lane == 0, 0.0, pltpu.roll(odd, 1, 1)).astype(BF)
                ref[z, at + 32:at + 96] = hid[i * 64:i * 64 + 64].astype(BF)


def beside(*parts):
    return parts[0] if len(parts) == 1 else jnp.concatenate(parts, axis=1)


def pair_rows(*places):
    return lambda m: beside(*[ref[z, m * 128:m * 128 + 160] for ref, z in places])


def second_section(w2t, planes, cot_ref, z, rows_c, rows_a, put):
    lane = lax.broadcasted_iota(jnp.int32, (64, LANES), 1)
    rows_c[...] = cot_ref[:, z].astype(F32).reshape(512, LANES)
    for y in range(8):
        acc = nn(w2t[0], planes[0][0][planes[0][1], y * 192:y * 192 + 288])
        acc += nn(w2t[1], planes[1][0][planes[1][1], y * 192:y * 192 + 288])
        acc += nn(w2t[2], planes[2][0][planes[2][1], y * 192:y * 192 + 288])
        rows_a[pl.ds(y, 64, stride=8), :] = leaky(acc)
        delta = rows_c[pl.ds(y, 64, stride=8), :] * jnp.where(acc > 0, 1.0, SLOPE)
        left = jnp.where(lane == LANES - 1, 0.0, pltpu.roll(delta, LANES - 1, 1))
        put(y, delta.astype(BF), left.astype(BF))


def own_kernel(v_ref, w1_ref, e_ref, w2_ref, sel, t1, w2t, lmat, d_ref, h_ref, stage, w1s):
    lane = lax.broadcasted_iota(jnp.int32, (512, LANES), 1)
    row = lax.broadcasted_iota(jnp.int32, (512, LANES), 0)
    base = row - 4 * lane
    for r in range(4):
        sel[:, r * LANES:(r + 1) * LANES] = jnp.where(base == r, 1.0, 0.0).astype(BF)
    for j in range(27):
        w1s[j // 9, (j % 9) * 4:(j % 9) * 4 + 4, :] = w1_ref[j].astype(F32)
    for dz in range(3):
        taps = tn(w1s[dz, 0:36].astype(BF), e_ref[...]).astype(BF)
        for b in range(4):
            t1[dz, b * 32:(b + 1) * 32, :] = taps[:, b * 256:b * 256 + 160]
    eye = jnp.where(lax.broadcasted_iota(jnp.int32, (64, 64), 0) == lax.broadcasted_iota(jnp.int32, (64, 64), 1), 1.0, 0.0).astype(BF)
    step = lax.broadcasted_iota(jnp.int32, (64, LANES), 1) - lax.broadcasted_iota(jnp.int32, (64, LANES), 0)
    to_low = jnp.where(step == 0, 1.0, 0.0).astype(BF)
    to_high = jnp.where(step == 64, 1.0, 0.0).astype(BF)
    lmat[...] = jnp.zeros_like(lmat)
    for dz in range(3):
        w2 = w2_ref[dz].astype(BF)
        w2t[dz] = nt(eye, w2).astype(BF)
        low, high = nn(w2, to_low), nn(w2, to_high)
        tap = lambda half, dy, dx: half[(dy * 3 + dx) * 32:(dy * 3 + dx) * 32 + 32]
        at = dz * 128
        lmat[at:at + 32, 0:128] = tap(low, 1, 1).astype(BF)
        lmat[at + 32:at + 64, 0:128] = (tap(low, 1, 2) + tap(high, 1, 0)).astype(BF)
        lmat[at + 64:at + 96, 0:128] = tap(low, 2, 1).astype(BF)
        lmat[at + 96:at + 128, 0:128] = (tap(low, 2, 2) + tap(high, 2, 0)).astype(BF)
        lmat[at + 64:at + 96, 128:256] = tap(low, 0, 1).astype(BF)
        lmat[at + 96:at + 128, 128:256] = (tap(low, 0, 2) + tap(high, 0, 0)).astype(BF)
    stage[...] = jnp.zeros_like(stage)
    repack(v_ref, 0, 4, sel, stage, d_ref, 0)
    repack(v_ref, 4, 4, sel, stage, d_ref, 4)
    first_section(t1, [pair_rows((d_ref, 1 + dz), (d_ref, 3 + dz)) for dz in range(3)], [(h_ref, 0), (h_ref, 1)])
    first_section(t1, [pair_rows((d_ref, 5 + dz)) for dz in range(3)], [(h_ref, 2)])


def halo_kernel(vh_ref, cot_ref, sel, t1, w2t, d_ref, h_ref, dl_ref, hl_ref, d2_ref, edge_ref, a0_ref, stage, rows_c, rows_a):
    stage[...] = jnp.zeros_like(stage)
    repack(vh_ref, 0, 3, sel, stage, dl_ref, 0)
    first_section(t1, [pair_rows((dl_ref, 0), (dl_ref, 2)), pair_rows((dl_ref, 1), (d_ref, 0)), pair_rows((dl_ref, 2), (d_ref, 1))],
                  [(hl_ref, 0), (hl_ref, 1)])
    d2_ref[1024:1152] = jnp.zeros((128, LANES), BF)

    def put(y, delta, left):
        d2_ref[y * 128:y * 128 + 64] = delta
        d2_ref[y * 128 + 64:y * 128 + 128] = left
        edge_ref[y * 64:y * 64 + 64] = delta

    second_section(w2t, [(hl_ref, 0), (hl_ref, 1), (h_ref, 0)], cot_ref, 0, rows_c, rows_a, put)
    a0_ref[...] = rows_a[...].astype(BF).reshape(64, 8, LANES)


def slopes(ref, z, m):
    parts = [jnp.where(ref[z, (2 * m + i + 1) * 96 + 32:(2 * m + i + 1) * 96 + 96].astype(F32) > 0, 1.0, SLOPE) for i in range(2)]
    return jnp.concatenate(parts, axis=0)


def inner_kernel(cot_ref, w2t, lmat, d_ref, h_ref, dl_ref, hl_ref, d2_ref, a0_ref,
                 act_ref, g2_ref, g1_ref, grad_ref, d2n, d1, rows_c, rows_a):
    d2n[1024:1152] = jnp.zeros((128, LANES), BF)

    def put(y, delta, left):
        d2n[y * 128:y * 128 + 64] = delta
        d2n[y * 128 + 64:y * 128 + 128] = left

    second_section(w2t, [(h_ref, 0), (h_ref, 1), (h_ref, 2)], cot_ref, 1, rows_c, rows_a, put)
    act_ref[:, 0] = a0_ref[...]
    act_ref[:, 1] = rows_a[...].astype(BF).reshape(64, 8, LANES)
    lower = [(hl_ref, 0), (hl_ref, 1), (h_ref, 0)]
    for dz in range(3):
        acc = jnp.zeros((288, LANES), F32)
        ref, z = lower[dz]
        for y in range(8):
            a = beside(ref[z, y * 192:y * 192 + 288], h_ref[dz, y * 192:y * 192 + 288])
            b = beside(d2_ref[y * 128:y * 128 + 128], d2n[y * 128:y * 128 + 128])
            acc += nt(a, b)
        g2_ref[dz * 288:dz * 288 + 288] = acc
    g2_ref[864:872] = jnp.zeros((8, LANES), F32)
    for m in range(8):
        rows = slice(m * 128, m * 128 + 128)
        r0 = nn(lmat[128:384], d2_ref[m * 128:m * 128 + 256])
        r1 = nn(lmat[...], d2n[m * 128:m * 128 + 256])
        d1[0, rows] = (r0[0:128] * slopes(hl_ref, 1, m)).astype(BF)
        d1[1, rows] = ((r0[128:256] + r1[0:128]) * slopes(h_ref, 0, m)).astype(BF)
        d1[2, rows] = (r1[128:256] * slopes(h_ref, 1, m)).astype(BF)
        grad_ref[rows] = r1[256:384]
    lower = [(dl_ref, 2), (d_ref, 0), (d_ref, 1)]
    for dz in range(3):
        acc = jnp.zeros((128, 160), F32)
        two, one = pair_rows(lower[dz], (d_ref, 1 + dz)), pair_rows((d_ref, 3 + dz))
        for m in range(8):
            rows = slice(m * 128, m * 128 + 128)
            acc += nt(beside(d1[0, rows], d1[1, rows]), two(m))
            acc += nt(d1[2, rows], one(m))
        g1_ref[dz] = acc


def edge_kernel(share, packed, above_ref, lmat, d_ref, h_ref, g2_ref, g1_ref, grad_ref, out_ref, d2h, d1):
    lane = lax.broadcasted_iota(jnp.int32, (64, LANES), 1)
    d2h[1024:1152] = jnp.zeros((128, LANES), BF)
    for y in range(8):
        low = above_ref[y * 64:y * 64 + 64]
        left = jnp.where(lane == LANES - 1, 0.0, pltpu.roll(low.astype(F32), LANES - 1, 1))
        d2h[y * 128:y * 128 + 64] = low
        d2h[y * 128 + 64:y * 128 + 128] = left.astype(BF)
    for m in range(8):
        rows = slice(m * 128, m * 128 + 128)
        grad = grad_ref[rows] + nn(lmat[0:128], d2h[m * 128:m * 128 + 256])
        d1[rows] = (grad * slopes(h_ref, 2, m)).astype(BF)
    lane = lax.broadcasted_iota(jnp.int32, (32, LANES), 1)
    total = jnp.zeros((32, LANES), F32)
    for dz in range(3):
        acc = g1_ref[dz]
        rows_of = pair_rows((d_ref, 5 + dz))
        for m in range(8):
            acc += nt(d1[m * 128:m * 128 + 128], rows_of(m))
        wide = (acc[:, 0:128], jnp.concatenate([acc[:, 128:160], jnp.zeros((128, 96), F32)], axis=1))
        for dy in range(3):
            to = (dz * 3 + dy) * 12
            part = jnp.zeros((32, LANES), F32)
            for i in range(2):
                for p in range(2):
                    y = 2 * i + dy
                    block = wide[y // 4][(2 * i + p) * 32:(2 * i + p) * 32 + 32]
                    shift = (to - ((y % 4) * 32 + 8 * p)) % LANES
                    part += block if shift == 0 else pltpu.roll(block, shift, 1)
            total = jnp.where((lane >= to) & (lane < to + 12), part, total)
    if not packed:
        out_ref[...] = total
        return
    count = share // 64
    low = lax.broadcasted_iota(jnp.int32, (14, LANES), 1) < 64
    for k in range(32):
        even = g2_ref[pl.ds(count * k, 14, stride=2), :]
        odd = g2_ref[pl.ds(count * k + 1, 14, stride=2), :]
        out_ref[k, 0:14] = jnp.where(low, even, pltpu.roll(odd, 64, 1))
        out_ref[k, 14:15] = total[k:k + 1]
        out_ref[k, 15:16] = jnp.zeros((1, LANES), F32)


def spread_kernel(count, full_ref, kernel_ref, first_ref, lines):
    for k in range(32):
        x = full_ref[k]
        lines[pl.ds(count * k, 14, stride=2), :] = x[0:14]
        lines[pl.ds(count * k + 1, 13, stride=2), :] = pltpu.roll(x, 64, 1)[0:13]
    kernel_ref[...] = lines[0:864, 0:64]
    columns = jnp.concatenate([full_ref[k, 14:15] for k in range(32)] + [jnp.zeros((96, LANES), F32)], axis=0)
    turned = columns.T
    for j in range(27):
        first_ref[j] = turned[j * 4:j * 4 + 4, 0:32]


VMEM = pl.BlockSpec(memory_space=pltpu.VMEM)


def call(kernel, outs, scratch, args):
    return pl.pallas_call(
        kernel,
        out_shape=[pltpu.VMEM(s, t) if stays else jax.ShapeDtypeStruct(s, t) for s, t, stays in outs],
        in_specs=[VMEM] * len(args),
        out_specs=[VMEM] * len(outs),
        scratch_shapes=[pltpu.VMEM(s, t) for s, t in scratch],
        compiler_params=pltpu.CompilerParams(vmem_limit_bytes=40 * 1024 * 1024),
    )(*args)


def stay(*arrays):
    return [pltpu.with_memory_space_constraint(a, pltpu.VMEM) for a in arrays]


def gather(values, count):
    wide = jnp.broadcast_to(values[None], (count,) + values.shape)
    return lax.all_to_all(wide, AXES, 0, 0, tiled=True)


def shards(volumes, first_kernel, second_kernel, cotangent, first_moment, second_moment):
    count = lax.axis_size(AXES)
    share = first_moment.shape[0]
    packed = count == 32 and share == 1728
    below = along(volumes[0, :, -3:], "space", 1)
    deep = lambda n: ((n, 1056, LANES), BF, True)
    hidden = lambda n: ((n, 1632, LANES), BF, True)
    sel, t1, w2t, lmat, d, h = call(
        own_kernel,
        [((512, 512), BF, True), ((3, 128, 160), BF, True), ((3, 64, 288), BF, True), ((384, 256), BF, True), deep(8), hidden(3)],
        [((4, 1056, LANES), F32), ((3, 40, 32), F32)],
        (volumes[0], first_kernel.reshape(27, 4, 32), jnp.asarray(spread_taps(), BF), second_kernel.reshape(3, 288, 64)),
    )
    sel, t1, w2t, lmat, d, h = stay(sel, t1, w2t, lmat, d, h)
    dl, hl, d2, edge, a0 = call(
        halo_kernel,
        [deep(3), hidden(2), ((1152, LANES), BF, True), ((512, LANES), BF, False), ((64, 8, LANES), BF, True)],
        [((3, 1056, LANES), F32), ((512, LANES), F32), ((512, LANES), F32)],
        (below, cotangent[0], sel, t1, w2t, d, h),
    )
    above = along(edge, "space", -1)
    dl, hl, d2, a0 = stay(dl, hl, d2, a0)
    act, g2, g1, grad = call(
        inner_kernel,
        [((64, 2, 8, LANES), BF, False), ((872, LANES), F32, packed), ((3, 128, 160), F32, True), ((1024, LANES), F32, True)],
        [((1152, LANES), BF), ((3, 1024, LANES), BF), ((512, LANES), F32), ((512, LANES), F32)],
        (cotangent[0], w2t, lmat, d, h, dl, hl, d2, a0),
    )
    g1, grad = stay(g1, grad)
    if packed:
        (g2,) = stay(g2)
    (out,) = call(
        functools.partial(edge_kernel, share, packed),
        [((32, 16, LANES) if packed else (32, LANES), F32, False)],
        [((1152, LANES), BF), ((1024, LANES), BF)],
        (above, lmat, d, h, g2, g1, grad),
    )
    if packed:
        both = lax.all_to_all(out, AXES, 0, 0, tiled=True).sum(0).reshape(-1)
    else:
        one = out[:, :108].T.reshape(-1)
        one = jnp.pad(one, (0, -one.shape[0] % count)).reshape(count, -1)
        both = jnp.concatenate([g2[:864, :64].reshape(count, share), one], axis=1)
        both = lax.all_to_all(both, AXES, 0, 0, tiled=True).sum(0)
    grad_share = both[:share]
    offset = lax.axis_index(AXES) * share
    new_first = BETA_FIRST * first_moment + (1.0 - BETA_FIRST) * grad_share
    new_second = BETA_SECOND * second_moment + (1.0 - BETA_SECOND) * grad_share * grad_share
    kernel_share = lax.dynamic_slice_in_dim(second_kernel.reshape(-1), offset, share, 0)
    updated = kernel_share - LEARN_RATE * new_first / (jnp.sqrt(new_second) + EPSILON)
    send = jnp.concatenate([updated, both[share:]])
    if packed:
        full = gather(send.reshape(16, LANES), count)
        new_kernel, first_gradient = call(
            functools.partial(spread_kernel, share // 64),
            [((864, 64), F32, False), ((27, 4, 32), F32, False)], [((880, LANES), F32)], (full,))
    else:
        full = gather(send, count)
        new_kernel = full[:, :share]
        first_gradient = full[:, share:].reshape(-1)[:first_kernel.size]
    return (act[None], first_gradient.reshape(first_kernel.shape), new_kernel.reshape(second_kernel.shape), new_first, new_second)


def solution(mesh):
    field = P("dp", None, "space", None, None)
    flat = P(AXES)
    return jax.shard_map(
        shards, mesh=mesh, in_specs=(field, P(), P(), field, flat, flat),
        out_specs=(field, P(), P(), flat, flat), check_vma=False)
```

```python
import functools
import jax
import jax.numpy as jnp
import numpy as np
from jax import lax
from jax.experimental import pallas as pl
from jax.experimental.pallas import tpu as pltpu
from jax.sharding import PartitionSpec as P

SLOPE = 0.3
BETA_FIRST = 0.9
BETA_SECOND = 0.999
LEARN_RATE = 0.001
EPSILON = 1e-08
BF = jnp.bfloat16
F32 = jnp.float32
AXES = ("dp", "space")
LANES = 128


def along(value, axis, steps):
    count = lax.axis_size(axis)
    first, last = (max(0, -steps), min(count, count - steps))
    return lax.ppermute(value, axis, [(source, source + steps) for source in range(first, last)])


def leaky(values):
    return jnp.where(values > 0, values, SLOPE * values)


def nn(a, b):
    return lax.dot_general(a, b, (((1,), (0,)), ((), ())), preferred_element_type=F32)


def nt(a, b):
    return lax.dot_general(a, b, (((1,), (1,)), ((), ())), preferred_element_type=F32)


def tn(a, b):
    return lax.dot_general(a, b, (((0,), (0,)), ((), ())), preferred_element_type=F32)


def spread_taps():
    table = np.zeros((3, 3, 4, 2, 2, 256), np.float32)
    for dy in range(3):
        for dx in range(3):
            for c in range(4):
                for row in range(2):
                    for p in range(2):
                        table[dy, dx, c, row, p, (2 * row + dy) * 32 + (2 * p + dx) * 4 + c] = 1
    return table.reshape(36, 1024)


def repack(source, first, count, sel, stage, out, to):
    x = jnp.concatenate([source[:, first + i].reshape(4 * 32, 512) for i in range(count)], axis=0)
    lane = lax.broadcasted_iota(jnp.int32, (32, LANES), 1)
    for r in range(4):
        part = nn(x, sel[:, r * LANES:(r + 1) * LANES])
        for i in range(count):
            for c in range(4):
                block = part[i * 128 + c * 32:i * 128 + c * 32 + 32]
                stage[i, pl.ds(32 + (r + 1) * 4 + c, 32, stride=32), :] = block
                if r == 3:
                    moved = jnp.where(lane == 0, 0.0, pltpu.roll(block, 1, 1))
                    stage[i, pl.ds(32 + c, 32, stride=32), :] = moved
    for i in range(count):
        out[to + i] = stage[i].astype(BF)


def first_section(t1, planes, outs):
    lane = lax.broadcasted_iota(jnp.int32, (32, LANES), 1)
    for ref, z in outs:
        ref[z, 0:96] = jnp.zeros((96, LANES), BF)
    for m in range(8):
        acc = nn(t1[0], planes[0](m))
        acc += nn(t1[1], planes[1](m))
        acc += nn(t1[2], planes[2](m))
        both = leaky(acc)
        for k, (ref, z) in enumerate(outs):
            hid = both[:, k * LANES:(k + 1) * LANES]
            for i in range(2):
                at = (2 * m + i + 1) * 96
                odd = hid[i * 64 + 32:i * 64 + 64]
                ref[z, at:at + 32] = jnp.where(lane == 0, 0.0, pltpu.roll(odd, 1, 1)).astype(BF)
                ref[z, at + 32:at + 96] = hid[i * 64:i * 64 + 64].astype(BF)


def beside(*parts):
    return parts[0] if len(parts) == 1 else jnp.concatenate(parts, axis=1)


def pair_rows(*places):
    return lambda m: beside(*[ref[z, m * 128:m * 128 + 160] for ref, z in places])


def second_section(w2t, planes, cot_ref, z, rows_c, rows_a, put):
    lane = lax.broadcasted_iota(jnp.int32, (64, LANES), 1)
    rows_c[...] = cot_ref[:, z].astype(F32).reshape(512, LANES)
    for y in range(8):
        acc = nn(w2t[0], planes[0][0][planes[0][1], y * 192:y * 192 + 288])
        acc += nn(w2t[1], planes[1][0][planes[1][1], y * 192:y * 192 + 288])
        acc += nn(w2t[2], planes[2][0][planes[2][1], y * 192:y * 192 + 288])
        rows_a[pl.ds(y, 64, stride=8), :] = leaky(acc)
        delta = rows_c[pl.ds(y, 64, stride=8), :] * jnp.where(acc > 0, 1.0, SLOPE)
        left = jnp.where(lane == LANES - 1, 0.0, pltpu.roll(delta, LANES - 1, 1))
        put(y, delta.astype(BF), left.astype(BF))


def own_kernel(v_hbm, w1_hbm, e_hbm, w2_hbm, cot_hbm, sel, t1, w2t, lmat, d_ref, h_ref, cot_ref,
               stage, w1s, v_ref, w1_ref, e_ref, w2_ref, sems):
    moves = [pltpu.make_async_copy(source, target, sems.at[i]) for i, (source, target) in enumerate((
        (w1_hbm, w1_ref), (e_hbm, e_ref), (w2_hbm, w2_ref),
        (v_hbm.at[:, 0:4], v_ref.at[:, 0:4]), (v_hbm.at[:, 4:8], v_ref.at[:, 4:8]), (cot_hbm, cot_ref)))]
    for move in moves:
        move.start()
    lane = lax.broadcasted_iota(jnp.int32, (512, LANES), 1)
    row = lax.broadcasted_iota(jnp.int32, (512, LANES), 0)
    base = row - 4 * lane
    for r in range(4):
        sel[:, r * LANES:(r + 1) * LANES] = jnp.where(base == r, 1.0, 0.0).astype(BF)
    stage[...] = jnp.zeros_like(stage)
    moves[0].wait()
    moves[1].wait()
    for j in range(27):
        w1s[j // 9, (j % 9) * 4:(j % 9) * 4 + 4, :] = w1_ref[j].astype(F32)
    for dz in range(3):
        taps = tn(w1s[dz, 0:36].astype(BF), e_ref[...]).astype(BF)
        for b in range(4):
            t1[dz, b * 32:(b + 1) * 32, :] = taps[:, b * 256:b * 256 + 160]
    eye = jnp.where(lax.broadcasted_iota(jnp.int32, (64, 64), 0) == lax.broadcasted_iota(jnp.int32, (64, 64), 1), 1.0, 0.0).astype(BF)
    step = lax.broadcasted_iota(jnp.int32, (64, LANES), 1) - lax.broadcasted_iota(jnp.int32, (64, LANES), 0)
    to_low = jnp.where(step == 0, 1.0, 0.0).astype(BF)
    to_high = jnp.where(step == 64, 1.0, 0.0).astype(BF)
    lmat[...] = jnp.zeros_like(lmat)
    moves[2].wait()
    for dz in range(3):
        w2 = w2_ref[dz].astype(BF)
        w2t[dz] = nt(eye, w2).astype(BF)
        low, high = nn(w2, to_low), nn(w2, to_high)
        tap = lambda half, dy, dx: half[(dy * 3 + dx) * 32:(dy * 3 + dx) * 32 + 32]
        at = dz * 128
        lmat[at:at + 32, 0:128] = tap(low, 1, 1).astype(BF)
        lmat[at + 32:at + 64, 0:128] = (tap(low, 1, 2) + tap(high, 1, 0)).astype(BF)
        lmat[at + 64:at + 96, 0:128] = tap(low, 2, 1).astype(BF)
        lmat[at + 96:at + 128, 0:128] = (tap(low, 2, 2) + tap(high, 2, 0)).astype(BF)
        lmat[at + 64:at + 96, 128:256] = tap(low, 0, 1).astype(BF)
        lmat[at + 96:at + 128, 128:256] = (tap(low, 0, 2) + tap(high, 0, 0)).astype(BF)
    moves[3].wait()
    repack(v_ref, 0, 4, sel, stage, d_ref, 0)
    moves[4].wait()
    repack(v_ref, 4, 4, sel, stage, d_ref, 4)
    first_section(t1, [pair_rows((d_ref, 1 + dz), (d_ref, 3 + dz)) for dz in range(3)], [(h_ref, 0), (h_ref, 1)])
    first_section(t1, [pair_rows((d_ref, 5 + dz)) for dz in range(3)], [(h_ref, 2)])
    moves[5].wait()


def halo_kernel(vh_ref, cot_ref, sel, t1, w2t, d_ref, h_ref, dl_ref, hl_ref, d2_ref, edge_ref, a0_ref, stage, rows_c, rows_a):
    stage[...] = jnp.zeros_like(stage)
    repack(vh_ref, 0, 3, sel, stage, dl_ref, 0)
    first_section(t1, [pair_rows((dl_ref, 0), (dl_ref, 2)), pair_rows((dl_ref, 1), (d_ref, 0)), pair_rows((dl_ref, 2), (d_ref, 1))],
                  [(hl_ref, 0), (hl_ref, 1)])
    d2_ref[1024:1152] = jnp.zeros((128, LANES), BF)

    def put(y, delta, left):
        d2_ref[y * 128:y * 128 + 64] = delta
        d2_ref[y * 128 + 64:y * 128 + 128] = left
        edge_ref[y * 64:y * 64 + 64] = delta

    second_section(w2t, [(hl_ref, 0), (hl_ref, 1), (h_ref, 0)], cot_ref, 0, rows_c, rows_a, put)
    a0_ref[...] = rows_a[...].astype(BF).reshape(64, 8, LANES)


def slopes(ref, z, m):
    parts = [jnp.where(ref[z, (2 * m + i + 1) * 96 + 32:(2 * m + i + 1) * 96 + 96].astype(F32) > 0, 1.0, SLOPE) for i in range(2)]
    return jnp.concatenate(parts, axis=0)


def inner_kernel(share, packed, cot_ref, w2t, lmat, d_ref, h_ref, dl_ref, hl_ref, d2_ref, a0_ref,
                 act_ref, out_ref, g1_ref, grad_ref, g2_ref, d2n, d1, rows_c, rows_a):
    d2n[1024:1152] = jnp.zeros((128, LANES), BF)

    def put(y, delta, left):
        d2n[y * 128:y * 128 + 64] = delta
        d2n[y * 128 + 64:y * 128 + 128] = left

    second_section(w2t, [(h_ref, 0), (h_ref, 1), (h_ref, 2)], cot_ref, 1, rows_c, rows_a, put)
    act_ref[:, 0] = a0_ref[...]
    act_ref[:, 1] = rows_a[...].astype(BF).reshape(64, 8, LANES)
    lower = [(hl_ref, 0), (hl_ref, 1), (h_ref, 0)]
    for dz in range(3):
        acc = jnp.zeros((288, LANES), F32)
        ref, z = lower[dz]
        for y in range(8):
            a = beside(ref[z, y * 192:y * 192 + 288], h_ref[dz, y * 192:y * 192 + 288])
            b = beside(d2_ref[y * 128:y * 128 + 128], d2n[y * 128:y * 128 + 128])
            acc += nt(a, b)
        g2_ref[dz * 288:dz * 288 + 288] = acc
    g2_ref[864:872] = jnp.zeros((8, LANES), F32)
    if packed:
        count = share // 64
        low = lax.broadcasted_iota(jnp.int32, (14, LANES), 1) < 64
        for k in range(32):
            even = g2_ref[pl.ds(count * k, 14, stride=2), :]
            odd = g2_ref[pl.ds(count * k + 1, 14, stride=2), :]
            out_ref[k * 16:k * 16 + 14] = jnp.where(low, even, pltpu.roll(odd, 64, 1))
    else:
        out_ref[...] = g2_ref[...]
    for m in range(8):
        rows = slice(m * 128, m * 128 + 128)
        r0 = nn(lmat[128:384], d2_ref[m * 128:m * 128 + 256])
        r1 = nn(lmat[...], d2n[m * 128:m * 128 + 256])
        d1[0, rows] = (r0[0:128] * slopes(hl_ref, 1, m)).astype(BF)
        d1[1, rows] = ((r0[128:256] + r1[0:128]) * slopes(h_ref, 0, m)).astype(BF)
        d1[2, rows] = (r1[128:256] * slopes(h_ref, 1, m)).astype(BF)
        grad_ref[rows] = r1[256:384]
    lower = [(dl_ref, 2), (d_ref, 0), (d_ref, 1)]
    for dz in range(3):
        acc = jnp.zeros((128, 160), F32)
        two, one = pair_rows(lower[dz], (d_ref, 1 + dz)), pair_rows((d_ref, 3 + dz))
        for m in range(8):
            rows = slice(m * 128, m * 128 + 128)
            acc += nt(beside(d1[0, rows], d1[1, rows]), two(m))
            acc += nt(d1[2, rows], one(m))
        g1_ref[dz] = acc


def edge_kernel(packed, above_ref, lmat, d_ref, h_ref, g1_ref, grad_ref, *rest):
    pay_ref, out_ref, d2h, d1, lines = rest if packed else (None,) + rest
    lane = lax.broadcasted_iota(jnp.int32, (64, LANES), 1)
    d2h[1024:1152] = jnp.zeros((128, LANES), BF)
    for y in range(8):
        low = above_ref[y * 64:y * 64 + 64]
        left = jnp.where(lane == LANES - 1, 0.0, pltpu.roll(low.astype(F32), LANES - 1, 1))
        d2h[y * 128:y * 128 + 64] = low
        d2h[y * 128 + 64:y * 128 + 128] = left.astype(BF)
    for m in range(8):
        rows = slice(m * 128, m * 128 + 128)
        grad = grad_ref[rows] + nn(lmat[0:128], d2h[m * 128:m * 128 + 256])
        d1[rows] = (grad * slopes(h_ref, 2, m)).astype(BF)
    lane = lax.broadcasted_iota(jnp.int32, (32, LANES), 1)
    total = jnp.zeros((32, LANES), F32)
    for dz in range(3):
        acc = g1_ref[dz]
        rows_of = pair_rows((d_ref, 5 + dz))
        for m in range(8):
            acc += nt(d1[m * 128:m * 128 + 128], rows_of(m))
        wide = (acc[:, 0:128], jnp.concatenate([acc[:, 128:160], jnp.zeros((128, 96), F32)], axis=1))
        for dy in range(3):
            to = (dz * 3 + dy) * 12
            part = jnp.zeros((32, LANES), F32)
            for i in range(2):
                for p in range(2):
                    y = 2 * i + dy
                    block = wide[y // 4][(2 * i + p) * 32:(2 * i + p) * 32 + 32]
                    shift = (to - ((y % 4) * 32 + 8 * p)) % LANES
                    part += block if shift == 0 else pltpu.roll(block, shift, 1)
            total = jnp.where((lane >= to) & (lane < to + 12), part, total)
    if not packed:
        out_ref[...] = total
        return
    lines[...] = pay_ref[...]
    lines[pl.ds(14, 32, stride=16), :] = total
    lines[pl.ds(15, 32, stride=16), :] = total - total.astype(BF).astype(F32)
    out_ref[...] = lines[...].astype(BF).reshape(32, 16, LANES)


def spread_kernel(count, full_ref, old_ref, kernel_ref, first_ref, lines):
    columns = []
    for k in range(32):
        x = full_ref[k].astype(F32)
        lines[pl.ds(count * k, 14, stride=2), :] = x[0:14]
        lines[pl.ds(count * k + 1, 13, stride=2), :] = pltpu.roll(x, 64, 1)[0:13]
        columns.append(x[14:15] + x[15:16])
    kernel_ref[...] = old_ref[...] - lines[0:864, 0:64]
    turned = jnp.concatenate(columns + [jnp.zeros((96, LANES), F32)], axis=0).T
    for j in range(27):
        first_ref[j] = turned[j * 4:j * 4 + 4, 0:32]


VMEM = pl.BlockSpec(memory_space=pltpu.VMEM)
HBM = pl.BlockSpec(memory_space=pltpu.HBM)
DMA = pltpu.SemaphoreType.DMA


def call(kernel, outs, scratch, args, at=VMEM):
    return pl.pallas_call(
        kernel,
        out_shape=[pltpu.VMEM(s, t) if stays else jax.ShapeDtypeStruct(s, t) for s, t, stays in outs],
        in_specs=[at] * len(args),
        out_specs=[VMEM] * len(outs),
        scratch_shapes=[DMA(s) if t is DMA else pltpu.VMEM(s, t) for s, t in scratch],
        compiler_params=pltpu.CompilerParams(vmem_limit_bytes=40 * 1024 * 1024),
    )(*args)


def stay(*arrays):
    return [pltpu.with_memory_space_constraint(a, pltpu.VMEM) for a in arrays]


def stay_out(arrays):
    return [pltpu.with_memory_space_constraint(a, pltpu.HBM) for a in arrays]


def gather(values, count):
    wide = jnp.broadcast_to(values[None], (count,) + values.shape)
    return lax.all_to_all(wide, AXES, 0, 0, tiled=True)


def shards(volumes, first_kernel, second_kernel, cotangent, first_moment, second_moment):
    count = lax.axis_size(AXES)
    share = first_moment.shape[0]
    packed = count == 32 and share == 1728
    below = along(volumes[0, :, -3:], "space", 1)
    deep = lambda n: ((n, 1056, LANES), BF, True)
    hidden = lambda n: ((n, 1632, LANES), BF, True)
    sel, t1, w2t, lmat, d, h, cot = call(
        own_kernel,
        [((512, 512), BF, True), ((3, 128, 160), BF, True), ((3, 64, 288), BF, True), ((384, 256), BF, True), deep(8), hidden(3), ((64, 2, 8, LANES), BF, True)],
        [((4, 1056, LANES), F32), ((3, 40, 32), F32), ((4, 8, 32, 512), BF), ((27, 4, 32), BF), ((36, 1024), BF), ((3, 288, 64), F32), ((6,), DMA)],
        stay_out((volumes[0], first_kernel.reshape(27, 4, 32), jnp.asarray(spread_taps(), BF), second_kernel.reshape(3, 288, 64), cotangent[0])), HBM,
    )
    sel, t1, w2t, lmat, d, h, cot = stay(sel, t1, w2t, lmat, d, h, cot)
    dl, hl, d2, edge, a0 = call(
        halo_kernel,
        [deep(3), hidden(2), ((1152, LANES), BF, True), ((512, LANES), BF, False), ((64, 8, LANES), BF, True)],
        [((3, 1056, LANES), F32), ((512, LANES), F32), ((512, LANES), F32)],
        (below, cot, sel, t1, w2t, d, h),
    )
    above = along(edge, "space", -1)
    dl, hl, d2, a0 = stay(dl, hl, d2, a0)
    act, g2, g1, grad = call(
        functools.partial(inner_kernel, share, packed),
        [((64, 2, 8, LANES), BF, False), ((512, LANES) if packed else (872, LANES), F32, packed), ((3, 128, 160), F32, True), ((1024, LANES), F32, True)],
        [((872, LANES), F32), ((1152, LANES), BF), ((3, 1024, LANES), BF), ((512, LANES), F32), ((512, LANES), F32)],
        (cot, w2t, lmat, d, h, dl, hl, d2, a0),
    )
    g1, grad = stay(g1, grad)
    if packed:
        (g2,) = stay(g2)
    (out,) = call(
        functools.partial(edge_kernel, packed),
        [((32, 16, LANES), BF, False) if packed else ((32, LANES), F32, False)],
        [((1152, LANES), BF), ((1024, LANES), BF), ((512, LANES), F32)],
        (above, lmat, d, h, g1, grad) + ((g2,) if packed else ()),
    )
    if packed:
        both = lax.all_to_all(out, AXES, 0, 0, tiled=True).astype(F32).sum(0)
        one = both[14] + both[15]
        both = both.reshape(-1)
    else:
        one = out[:, :108].T.reshape(-1)
        one = jnp.pad(one, (0, -one.shape[0] % count)).reshape(count, -1)
        both = jnp.concatenate([g2[:864, :64].reshape(count, share), one], axis=1)
        both = lax.all_to_all(both, AXES, 0, 0, tiled=True).sum(0)
    grad_share = both[:share]
    new_first = BETA_FIRST * first_moment + (1.0 - BETA_FIRST) * grad_share
    new_second = BETA_SECOND * second_moment + (1.0 - BETA_SECOND) * grad_share * grad_share
    change = LEARN_RATE * new_first / (jnp.sqrt(new_second) + EPSILON)
    if packed:
        tail = jnp.stack([one, one - lax.reduce_precision(one, 8, 7)])
        send = jnp.concatenate([jnp.pad(change, (0, 64)).reshape(14, LANES), tail]).astype(BF)
        full = gather(send, count)
        new_kernel, first_gradient = call(
            functools.partial(spread_kernel, share // 64),
            [((864, 64), F32, False), ((27, 4, 32), F32, False)], [((880, LANES), F32)], (full, second_kernel.reshape(864, 64)))
    else:
        offset = lax.axis_index(AXES) * share
        kernel_share = lax.dynamic_slice_in_dim(second_kernel.reshape(-1), offset, share, 0)
        full = gather(jnp.concatenate([kernel_share - change, both[share:]]), count)
        new_kernel = full[:, :share]
        first_gradient = full[:, share:].reshape(-1)[:first_kernel.size]
    return (act[None], first_gradient.reshape(first_kernel.shape), new_kernel.reshape(second_kernel.shape), new_first, new_second)


def solution(mesh):
    field = P("dp", None, "space", None, None)
    flat = P(AXES)
    return jax.shard_map(
        shards, mesh=mesh, in_specs=(field, P(), P(), field, flat, flat),
        out_specs=(field, P(), P(), flat, flat), check_vma=False)
```

```python
import functools
import jax
import jax.numpy as jnp
import numpy as np
from jax import lax
from jax.experimental import pallas as pl
from jax.experimental.pallas import tpu as pltpu
from jax.sharding import PartitionSpec as P

SLOPE = 0.3
BETA_FIRST = 0.9
BETA_SECOND = 0.999
LEARN_RATE = 0.001
EPSILON = 1e-08
BF = jnp.bfloat16
F32 = jnp.float32
AXES = ("dp", "space")
LANES = 128
SLOTS = 20
REACH = 112
DEEP = 672


def along(value, axis, steps):
    count = lax.axis_size(axis)
    first, last = (max(0, -steps), min(count, count - steps))
    return lax.ppermute(value, axis, [(source, source + steps) for source in range(first, last)])


def leaky(values):
    return jnp.where(values > 0, values, SLOPE * values)


def nn(a, b):
    return lax.dot_general(a, b, (((1,), (0,)), ((), ())), preferred_element_type=F32)


def nt(a, b):
    return lax.dot_general(a, b, (((1,), (1,)), ((), ())), preferred_element_type=F32)


def tn(a, b):
    return lax.dot_general(a, b, (((0,), (0,)), ((), ())), preferred_element_type=F32)


def spread_taps():
    table = np.zeros((3, 3, 4, 2, 2, LANES), np.float32)
    for dy in range(3):
        for dx in range(3):
            for c in range(4):
                for row in range(2):
                    for p in range(2):
                        table[dy, dx, c, row, p, (2 * row + dy) * SLOTS + (2 * p + dx) * 4 + c] = 1
    return table.reshape(36, 512)


def repack(source, first, count, sel, stage, out, to):
    x = jnp.concatenate([source[:, first + i].reshape(4 * 32, 512) for i in range(count)], axis=0)
    lane = lax.broadcasted_iota(jnp.int32, (32, LANES), 1)
    for r in range(4):
        part = nn(x, sel[:, r * LANES:(r + 1) * LANES])
        for i in range(count):
            for c in range(4):
                block = part[i * 128 + c * 32:i * 128 + c * 32 + 32]
                stage[i, pl.ds(SLOTS + (r + 1) * 4 + c, 32, stride=SLOTS), :] = block
                if r == 3:
                    moved = jnp.where(lane == 0, 0.0, pltpu.roll(block, 1, 1))
                    stage[i, pl.ds(SLOTS + c, 32, stride=SLOTS), :] = moved
    for i in range(count):
        out[to + i] = stage[i].astype(BF)


def clear(stage):
    for i in range(stage.shape[0]):
        stage[i, 0:24] = jnp.zeros((24, LANES), F32)
        stage[i, 656:DEEP] = jnp.zeros((DEEP - 656, LANES), F32)


def first_section(t1, planes, outs):
    lane = lax.broadcasted_iota(jnp.int32, (32, LANES), 1)
    for ref, z in outs:
        ref[z, 0:96] = jnp.zeros((96, LANES), BF)
    for m in range(8):
        acc = nn(t1[0], planes[0](m))
        acc += nn(t1[1], planes[1](m))
        acc += nn(t1[2], planes[2](m))
        both = leaky(acc)
        for k, (ref, z) in enumerate(outs):
            hid = both[:, k * LANES:(k + 1) * LANES]
            for i in range(2):
                at = (2 * m + i + 1) * 96
                odd = hid[i * 64 + 32:i * 64 + 64]
                ref[z, at:at + 32] = jnp.where(lane == 0, 0.0, pltpu.roll(odd, 1, 1)).astype(BF)
                ref[z, at + 32:at + 96] = hid[i * 64:i * 64 + 64].astype(BF)


def beside(*parts):
    return parts[0] if len(parts) == 1 else jnp.concatenate(parts, axis=1)


def pair_rows(*places):
    return lambda m: beside(*[ref[z, m * 4 * SLOTS:m * 4 * SLOTS + REACH] for ref, z in places])


def second_section(w2t, planes, cot_ref, z, rows_c, rows_a, put):
    lane = lax.broadcasted_iota(jnp.int32, (64, LANES), 1)
    rows_c[...] = cot_ref[:, z].astype(F32).reshape(512, LANES)
    for y in range(8):
        acc = nn(w2t[0], planes[0][0][planes[0][1], y * 192:y * 192 + 288])
        acc += nn(w2t[1], planes[1][0][planes[1][1], y * 192:y * 192 + 288])
        acc += nn(w2t[2], planes[2][0][planes[2][1], y * 192:y * 192 + 288])
        rows_a[pl.ds(y, 64, stride=8), :] = leaky(acc)
        delta = rows_c[pl.ds(y, 64, stride=8), :] * jnp.where(acc > 0, 1.0, SLOPE)
        left = jnp.where(lane == LANES - 1, 0.0, pltpu.roll(delta, LANES - 1, 1))
        put(y, delta.astype(BF), left.astype(BF))


def own_kernel(v_hbm, w1_hbm, e_hbm, w2_hbm, cot_hbm, sel, t1, w2t, lmat, d_ref, h_ref, cot_ref, d2_ref, edge_ref, act_ref,
               stage, rows_c, rows_a, w1s, v_ref, w1_ref, e_ref, w2_ref, sems):
    moves = [pltpu.make_async_copy(source, target, sems.at[i]) for i, (source, target) in enumerate((
        (w1_hbm, w1_ref), (e_hbm, e_ref), (w2_hbm, w2_ref),
        (v_hbm.at[:, 0:4], v_ref.at[:, 0:4]), (v_hbm.at[:, 4:8], v_ref.at[:, 4:8]), (cot_hbm, cot_ref)))]
    for move in moves:
        move.start()
    lane = lax.broadcasted_iota(jnp.int32, (512, LANES), 1)
    row = lax.broadcasted_iota(jnp.int32, (512, LANES), 0)
    base = row - 4 * lane
    for r in range(4):
        sel[:, r * LANES:(r + 1) * LANES] = jnp.where(base == r, 1.0, 0.0).astype(BF)
    clear(stage)
    moves[0].wait()
    moves[1].wait()
    for j in range(27):
        w1s[j // 9, (j % 9) * 4:(j % 9) * 4 + 4, :] = w1_ref[j].astype(F32)
    for dz in range(3):
        taps = tn(w1s[dz, 0:36].astype(BF), e_ref[...]).astype(BF)
        for b in range(4):
            t1[dz, b * 32:(b + 1) * 32, :] = taps[:, b * LANES:b * LANES + REACH]
    eye = jnp.where(lax.broadcasted_iota(jnp.int32, (64, 64), 0) == lax.broadcasted_iota(jnp.int32, (64, 64), 1), 1.0, 0.0).astype(BF)
    step = lax.broadcasted_iota(jnp.int32, (64, LANES), 1) - lax.broadcasted_iota(jnp.int32, (64, LANES), 0)
    to_low = jnp.where(step == 0, 1.0, 0.0).astype(BF)
    to_high = jnp.where(step == 64, 1.0, 0.0).astype(BF)
    lmat[...] = jnp.zeros_like(lmat)
    moves[2].wait()
    for dz in range(3):
        w2 = w2_ref[dz].astype(BF)
        w2t[dz] = nt(eye, w2).astype(BF)
        low, high = nn(w2, to_low), nn(w2, to_high)
        tap = lambda half, dy, dx: half[(dy * 3 + dx) * 32:(dy * 3 + dx) * 32 + 32]
        at = dz * 128
        lmat[at:at + 32, 0:128] = tap(low, 1, 1).astype(BF)
        lmat[at + 32:at + 64, 0:128] = (tap(low, 1, 2) + tap(high, 1, 0)).astype(BF)
        lmat[at + 64:at + 96, 0:128] = tap(low, 2, 1).astype(BF)
        lmat[at + 96:at + 128, 0:128] = (tap(low, 2, 2) + tap(high, 2, 0)).astype(BF)
        lmat[at + 64:at + 96, 128:256] = tap(low, 0, 1).astype(BF)
        lmat[at + 96:at + 128, 128:256] = (tap(low, 0, 2) + tap(high, 0, 0)).astype(BF)
    moves[3].wait()
    repack(v_ref, 0, 4, sel, stage, d_ref, 0)
    moves[4].wait()
    repack(v_ref, 4, 4, sel, stage, d_ref, 4)
    first_section(t1, [pair_rows((d_ref, 1 + dz), (d_ref, 3 + dz)) for dz in range(3)], [(h_ref, 0), (h_ref, 1)])
    first_section(t1, [pair_rows((d_ref, 5 + dz)) for dz in range(3)], [(h_ref, 2)])
    moves[5].wait()
    d2_ref[1024:1152] = jnp.zeros((128, LANES), BF)

    def put(y, delta, left):
        d2_ref[y * 128:y * 128 + 64] = delta
        d2_ref[y * 128 + 64:y * 128 + 128] = left
        edge_ref[y * 64:y * 64 + 64] = delta

    second_section(w2t, [(h_ref, 0), (h_ref, 1), (h_ref, 2)], cot_ref, 1, rows_c, rows_a, put)
    act_ref[...] = rows_a[...].astype(BF).reshape(64, 8, LANES)


def slopes(ref, z, m):
    parts = [jnp.where(ref[z, (2 * m + i + 1) * 96 + 32:(2 * m + i + 1) * 96 + 96].astype(F32) > 0, 1.0, SLOPE) for i in range(2)]
    return jnp.concatenate(parts, axis=0)


def inner_kernel(share, packed, vh_ref, cot_ref, sel, t1, w2t, lmat, d_ref, h_ref, d2n, upper_ref,
                 act_ref, out_ref, g1_ref, grad_ref, dl_ref, hl_ref, stage, g2_ref, d2_ref, d1, rows_c, rows_a):
    clear(stage)
    repack(vh_ref, 0, 3, sel, stage, dl_ref, 0)
    first_section(t1, [pair_rows((dl_ref, 0), (dl_ref, 2)), pair_rows((dl_ref, 1), (d_ref, 0)), pair_rows((dl_ref, 2), (d_ref, 1))],
                  [(hl_ref, 0), (hl_ref, 1)])
    d2_ref[1024:1152] = jnp.zeros((128, LANES), BF)

    def put(y, delta, left):
        d2_ref[y * 128:y * 128 + 64] = delta
        d2_ref[y * 128 + 64:y * 128 + 128] = left

    second_section(w2t, [(hl_ref, 0), (hl_ref, 1), (h_ref, 0)], cot_ref, 0, rows_c, rows_a, put)
    act_ref[:, 0] = rows_a[...].astype(BF).reshape(64, 8, LANES)
    act_ref[:, 1] = upper_ref[...]
    lower = [(hl_ref, 0), (hl_ref, 1), (h_ref, 0)]
    for dz in range(3):
        acc = jnp.zeros((288, 64), F32)
        ref, z = lower[dz]
        for y in range(8):
            a = beside(ref[z, y * 192:y * 192 + 288], h_ref[dz, y * 192:y * 192 + 288])
            b = beside(d2_ref[y * 128:y * 128 + 64], d2n[y * 128:y * 128 + 64])
            acc += nt(a, b)
        g2_ref[dz * 288:dz * 288 + 288, 0:64] = acc
    g2_ref[864:872] = jnp.zeros((8, LANES), F32)
    if packed:
        count = share // 64
        low = lax.broadcasted_iota(jnp.int32, (14, LANES), 1) < 64
        for k in range(32):
            even = g2_ref[pl.ds(count * k, 14, stride=2), :]
            odd = g2_ref[pl.ds(count * k + 1, 14, stride=2), :]
            out_ref[k * 16:k * 16 + 14] = jnp.where(low, even, pltpu.roll(odd, 64, 1))
    else:
        out_ref[...] = g2_ref[...]
    for m in range(8):
        rows = slice(m * 128, m * 128 + 128)
        r = nn(lmat[...], beside(d2_ref[m * 128:m * 128 + 256], d2n[m * 128:m * 128 + 256]))
        r0, r1 = r[:, 0:LANES], r[:, LANES:2 * LANES]
        grad_ref[rows] = r0[0:128]
        d1[0, rows] = (r0[128:256] * slopes(hl_ref, 1, m)).astype(BF)
        d1[1, rows] = ((r0[256:384] + r1[0:128]) * slopes(h_ref, 0, m)).astype(BF)
        d1[2, rows] = (r1[128:256] * slopes(h_ref, 1, m)).astype(BF)
    lower = [(dl_ref, 2), (d_ref, 0), (d_ref, 1)]
    for dz in range(3):
        acc = jnp.zeros((128, REACH), F32)
        two, one = pair_rows(lower[dz], (d_ref, 1 + dz)), pair_rows((d_ref, 3 + dz))
        for m in range(8):
            rows = slice(m * 128, m * 128 + 128)
            acc += nt(beside(d1[0, rows], d1[1, rows]), two(m))
            acc += nt(d1[2, rows], one(m))
        g1_ref[dz] = acc

    @pl.when(lax.axis_index("space") == lax.axis_size("space") - 1)
    def _():
        for m in range(8):
            rows = slice(m * 128, m * 128 + 128)
            d1[0, rows] = (nn(lmat[256:384], d2n[m * 128:m * 128 + 256]) * slopes(h_ref, 2, m)).astype(BF)
        for dz in range(3):
            acc = g1_ref[dz]
            one = pair_rows((d_ref, 5 + dz))
            for m in range(8):
                acc += nt(d1[0, m * 128:m * 128 + 128], one(m))
            g1_ref[dz] = acc


def edge_kernel(packed, under_ref, lmat, dl_ref, hl_ref, g1_ref, grad_ref, *rest):
    pay_ref, out_ref, d2h, d1, lines = rest if packed else (None,) + rest
    lane = lax.broadcasted_iota(jnp.int32, (64, LANES), 1)
    d2h[1024:1152] = jnp.zeros((128, LANES), BF)
    for y in range(8):
        low = under_ref[y * 64:y * 64 + 64]
        left = jnp.where(lane == LANES - 1, 0.0, pltpu.roll(low.astype(F32), LANES - 1, 1))
        d2h[y * 128:y * 128 + 64] = low
        d2h[y * 128 + 64:y * 128 + 128] = left.astype(BF)
    for m in range(8):
        rows = slice(m * 128, m * 128 + 128)
        grad = grad_ref[rows] + nn(lmat[256:384], d2h[m * 128:m * 128 + 256])
        d1[rows] = (grad * slopes(hl_ref, 0, m)).astype(BF)
    lane = lax.broadcasted_iota(jnp.int32, (32, LANES), 1)
    total = jnp.zeros((32, LANES), F32)
    for dz in range(3):
        acc = g1_ref[dz]
        rows_of = pair_rows((dl_ref, dz))
        for m in range(8):
            acc += nt(d1[m * 128:m * 128 + 128], rows_of(m))
        wide = jnp.concatenate([acc, jnp.zeros((128, LANES - REACH), F32)], axis=1)
        for dy in range(3):
            to = (dz * 3 + dy) * 12
            part = jnp.zeros((32, LANES), F32)
            for i in range(2):
                for p in range(2):
                    block = wide[(2 * i + p) * 32:(2 * i + p) * 32 + 32]
                    shift = (to - ((2 * i + dy) * SLOTS + 8 * p)) % LANES
                    part += block if shift == 0 else pltpu.roll(block, shift, 1)
            total = jnp.where((lane >= to) & (lane < to + 12), part, total)
    if not packed:
        out_ref[...] = total
        return
    lines[...] = pay_ref[...]
    lines[pl.ds(14, 32, stride=16), :] = total
    lines[pl.ds(15, 32, stride=16), :] = total - total.astype(BF).astype(F32)
    out_ref[...] = lines[...].astype(BF).reshape(32, 16, LANES)


def spread_kernel(count, full_ref, old_ref, kernel_ref, first_ref, lines):
    columns = []
    for k in range(32):
        x = full_ref[k].astype(F32)
        lines[pl.ds(count * k, 14, stride=2), :] = x[0:14]
        lines[pl.ds(count * k + 1, 13, stride=2), :] = pltpu.roll(x, 64, 1)[0:13]
        columns.append(x[14:15] + x[15:16])
    kernel_ref[...] = old_ref[...] - lines[0:864, 0:64]
    turned = jnp.concatenate(columns + [jnp.zeros((96, LANES), F32)], axis=0).T
    for j in range(27):
        first_ref[j] = turned[j * 4:j * 4 + 4, 0:32]


VMEM = pl.BlockSpec(memory_space=pltpu.VMEM)
HBM = pl.BlockSpec(memory_space=pltpu.HBM)
DMA = pltpu.SemaphoreType.DMA


def call(kernel, outs, scratch, args, at=VMEM):
    return pl.pallas_call(
        kernel,
        out_shape=[pltpu.VMEM(s, t) if stays else jax.ShapeDtypeStruct(s, t) for s, t, stays in outs],
        in_specs=[at] * len(args),
        out_specs=[VMEM] * len(outs),
        scratch_shapes=[DMA(s) if t is DMA else pltpu.VMEM(s, t) for s, t in scratch],
        compiler_params=pltpu.CompilerParams(vmem_limit_bytes=32 * 1024 * 1024),
    )(*args)


def stay(*arrays):
    return [pltpu.with_memory_space_constraint(a, pltpu.VMEM) for a in arrays]


def stay_out(arrays):
    return [pltpu.with_memory_space_constraint(a, pltpu.HBM) for a in arrays]


def gather(values, count):
    wide = jnp.broadcast_to(values[None], (count,) + values.shape)
    return lax.all_to_all(wide, AXES, 0, 0, tiled=True)


def shards(volumes, first_kernel, second_kernel, cotangent, first_moment, second_moment):
    count = lax.axis_size(AXES)
    share = first_moment.shape[0]
    packed = count == 32 and share == 1728
    below = along(volumes[0, :, -3:], "space", 1)
    deep = lambda n: ((n, DEEP, LANES), BF, True)
    hidden = lambda n: ((n, 1632, LANES), BF, True)
    plane = ((64, 8, LANES), BF, True)
    spread = ((1152, LANES), BF)
    flat = ((512, LANES), F32)
    sel, t1, w2t, lmat, d, h, cot, d2, edge, upper = call(
        own_kernel,
        [((512, 512), BF, True), ((3, 128, REACH), BF, True), ((3, 64, 288), BF, True), ((384, 256), BF, True), deep(8), hidden(3),
         ((64, 2, 8, LANES), BF, True), spread + (True,), ((512, LANES), BF, False), plane],
        [((4, DEEP, LANES), F32), flat, flat, ((3, 40, 32), F32),
         ((4, 8, 32, 512), BF), ((27, 4, 32), BF), ((36, 512), BF), ((3, 288, 64), F32), ((6,), DMA)],
        stay_out((volumes[0], first_kernel.reshape(27, 4, 32), jnp.asarray(spread_taps(), BF), second_kernel.reshape(3, 288, 64), cotangent[0])), HBM,
    )
    cot, sel, t1, w2t, lmat, d, h, d2, upper = stay(cot, sel, t1, w2t, lmat, d, h, d2, upper)
    under = along(edge, "space", 1)
    act, g2, g1, grad, dl, hl = call(
        functools.partial(inner_kernel, share, packed),
        [((64, 2, 8, LANES), BF, False), ((512, LANES) if packed else (872, LANES), F32, packed), ((3, 128, REACH), F32, True),
         ((1024, LANES), F32, True), deep(3), hidden(2)],
        [((3, DEEP, LANES), F32), ((872, LANES), F32), spread, ((3, 1024, LANES), BF), flat, flat],
        [below, cot, sel, t1, w2t, lmat, d, h, d2, upper],
    )
    (out,) = call(
        functools.partial(edge_kernel, packed),
        [((32, 16, LANES), BF, False) if packed else ((32, LANES), F32, False)],
        [spread, ((1024, LANES), BF), flat],
        [under, lmat] + stay(dl, hl, g1, grad) + (stay(g2) if packed else []),
    )
    if packed:
        both = lax.all_to_all(out, AXES, 0, 0, tiled=True).astype(F32).sum(0)
        one = both[14] + both[15]
        both = both.reshape(-1)
    else:
        one = out[:, :108].T.reshape(-1)
        one = jnp.pad(one, (0, -one.shape[0] % count)).reshape(count, -1)
        both = jnp.concatenate([g2[:864, :64].reshape(count, share), one], axis=1)
        both = lax.all_to_all(both, AXES, 0, 0, tiled=True).sum(0)
    grad_share = both[:share]
    new_first = BETA_FIRST * first_moment + (1.0 - BETA_FIRST) * grad_share
    new_second = BETA_SECOND * second_moment + (1.0 - BETA_SECOND) * grad_share * grad_share
    change = LEARN_RATE * new_first / (jnp.sqrt(new_second) + EPSILON)
    if packed:
        tail = jnp.stack([one, one - lax.reduce_precision(one, 8, 7)])
        send = jnp.concatenate([jnp.pad(change, (0, 64)).reshape(14, LANES), tail]).astype(BF)
        full = gather(send, count)
        new_kernel, first_gradient = call(
            functools.partial(spread_kernel, share // 64),
            [((864, 64), F32, False), ((27, 4, 32), F32, False)], [((880, LANES), F32)], (full, second_kernel.reshape(864, 64)))
    else:
        offset = lax.axis_index(AXES) * share
        kernel_share = lax.dynamic_slice_in_dim(second_kernel.reshape(-1), offset, share, 0)
        full = gather(jnp.concatenate([kernel_share - change, both[share:]]), count)
        new_kernel = full[:, :share]
        first_gradient = full[:, share:].reshape(-1)[:first_kernel.size]
    return (act[None], first_gradient.reshape(first_kernel.shape), new_kernel.reshape(second_kernel.shape), new_first, new_second)


def solution(mesh):
    field = P("dp", None, "space", None, None)
    flat = P(AXES)
    return jax.shard_map(
        shards, mesh=mesh, in_specs=(field, P(), P(), field, flat, flat),
        out_specs=(field, P(), P(), flat, flat), check_vma=False)
```

```python
import functools
import jax
import jax.numpy as jnp
import numpy as np
from jax import lax
from jax.experimental import pallas as pl
from jax.experimental.pallas import tpu as pltpu
from jax.sharding import PartitionSpec as P

SLOPE = 0.3
BETA_FIRST = 0.9
BETA_SECOND = 0.999
LEARN_RATE = 0.001
EPSILON = 1e-08
BF = jnp.bfloat16
F32 = jnp.float32
AXES = ("dp", "space")
LANES = 128
SLOTS = 20
REACH = 112
DEEP = 672


def along(value, axis, steps):
    count = lax.axis_size(axis)
    first, last = (max(0, -steps), min(count, count - steps))
    return lax.ppermute(value, axis, [(source, source + steps) for source in range(first, last)])


def leaky(values):
    return jnp.where(values > 0, values, SLOPE * values)


def nn(a, b):
    return lax.dot_general(a, b, (((1,), (0,)), ((), ())), preferred_element_type=F32)


def nt(a, b):
    return lax.dot_general(a, b, (((1,), (1,)), ((), ())), preferred_element_type=F32)


def tn(a, b):
    return lax.dot_general(a, b, (((0,), (0,)), ((), ())), preferred_element_type=F32)


def spread_taps():
    table = np.zeros((3, 3, 4, 2, 2, LANES), np.float32)
    for dy in range(3):
        for dx in range(3):
            for c in range(4):
                for row in range(2):
                    for p in range(2):
                        table[dy, dx, c, row, p, (2 * row + dy) * SLOTS + (2 * p + dx) * 4 + c] = 1
    return table.reshape(36, 512)


def repack(source, first, count, sel, stage, out, to):
    x = jnp.concatenate([source[:, first + i].reshape(4 * 32, 512) for i in range(count)], axis=0)
    lane = lax.broadcasted_iota(jnp.int32, (32, LANES), 1)
    for r0 in range(0, 4, 2):
        parts = nn(x, sel[:, r0 * LANES:(r0 + 2) * LANES])
        for r in range(r0, r0 + 2):
            part = parts[:, (r - r0) * LANES:(r - r0 + 1) * LANES]
            for i in range(count):
                for c in range(4):
                    block = part[i * 128 + c * 32:i * 128 + c * 32 + 32]
                    stage[i, pl.ds(SLOTS + (r + 1) * 4 + c, 32, stride=SLOTS), :] = block
                    if r == 3:
                        moved = jnp.where(lane == 0, 0.0, pltpu.roll(block, 1, 1))
                        stage[i, pl.ds(SLOTS + c, 32, stride=SLOTS), :] = moved
    for i in range(count):
        out[to + i] = stage[i].astype(BF)


def clear(stage):
    for i in range(stage.shape[0]):
        stage[i, 0:24] = jnp.zeros((24, LANES), F32)
        stage[i, 656:DEEP] = jnp.zeros((DEEP - 656, LANES), F32)


def first_section(t1, planes, outs):
    lane = lax.broadcasted_iota(jnp.int32, (32, LANES), 1)
    for ref, z in outs:
        ref[z, 0:96] = jnp.zeros((96, LANES), BF)
    for m in range(8):
        acc = nn(t1[0], planes[0](m))
        acc += nn(t1[1], planes[1](m))
        acc += nn(t1[2], planes[2](m))
        both = leaky(acc)
        for k, (ref, z) in enumerate(outs):
            hid = both[:, k * LANES:(k + 1) * LANES]
            for i in range(2):
                at = (2 * m + i + 1) * 96
                odd = hid[i * 64 + 32:i * 64 + 64]
                ref[z, at:at + 32] = jnp.where(lane == 0, 0.0, pltpu.roll(odd, 1, 1)).astype(BF)
                ref[z, at + 32:at + 96] = hid[i * 64:i * 64 + 64].astype(BF)


def beside(*parts):
    return parts[0] if len(parts) == 1 else jnp.concatenate(parts, axis=1)


def pair_rows(*places):
    return lambda m: beside(*[ref[z, m * 4 * SLOTS:m * 4 * SLOTS + REACH] for ref, z in places])


def second_section(w2t, planes, cot_ref, z, rows_c, rows_a, put):
    lane = lax.broadcasted_iota(jnp.int32, (64, LANES), 1)
    rows_c[...] = cot_ref[:, z].astype(F32).reshape(512, LANES)
    for y in range(8):
        acc = nn(w2t[0], planes[0][0][planes[0][1], y * 192:y * 192 + 288])
        acc += nn(w2t[1], planes[1][0][planes[1][1], y * 192:y * 192 + 288])
        acc += nn(w2t[2], planes[2][0][planes[2][1], y * 192:y * 192 + 288])
        rows_a[pl.ds(y, 64, stride=8), :] = leaky(acc)
        delta = rows_c[pl.ds(y, 64, stride=8), :] * jnp.where(acc > 0, 1.0, SLOPE)
        left = jnp.where(lane == LANES - 1, 0.0, pltpu.roll(delta, LANES - 1, 1))
        put(y, delta.astype(BF), left.astype(BF))


def own_kernel(v_hbm, w1_hbm, e_hbm, w2_hbm, cot_hbm, sel, t1, w2t, lmat, d_ref, h_ref, cot_ref, d2_ref, edge_ref, act_ref,
               stage, rows_c, rows_a, w1s, v_ref, w1_ref, e_ref, w2_ref, sems):
    moves = [pltpu.make_async_copy(source, target, sems.at[i]) for i, (source, target) in enumerate((
        (w1_hbm, w1_ref), (e_hbm, e_ref), (w2_hbm, w2_ref),
        (v_hbm.at[:, 0:4], v_ref.at[:, 0:4]), (v_hbm.at[:, 4:8], v_ref.at[:, 4:8]), (cot_hbm, cot_ref)))]
    for move in moves:
        move.start()
    lane = lax.broadcasted_iota(jnp.int32, (512, LANES), 1)
    row = lax.broadcasted_iota(jnp.int32, (512, LANES), 0)
    base = row - 4 * lane
    for r in range(4):
        sel[:, r * LANES:(r + 1) * LANES] = jnp.where(base == r, 1.0, 0.0).astype(BF)
    clear(stage)
    moves[0].wait()
    moves[1].wait()
    for j in range(27):
        w1s[j // 9, (j % 9) * 4:(j % 9) * 4 + 4, :] = w1_ref[j].astype(F32)
    for dz in range(3):
        taps = tn(w1s[dz, 0:36].astype(BF), e_ref[...]).astype(BF)
        for b in range(4):
            t1[dz, b * 32:(b + 1) * 32, :] = taps[:, b * LANES:b * LANES + REACH]
    eye = jnp.where(lax.broadcasted_iota(jnp.int32, (64, 64), 0) == lax.broadcasted_iota(jnp.int32, (64, 64), 1), 1.0, 0.0).astype(BF)
    step = lax.broadcasted_iota(jnp.int32, (64, LANES), 1) - lax.broadcasted_iota(jnp.int32, (64, LANES), 0)
    to_low = jnp.where(step == 0, 1.0, 0.0).astype(BF)
    to_high = jnp.where(step == 64, 1.0, 0.0).astype(BF)
    lmat[...] = jnp.zeros_like(lmat)
    moves[2].wait()
    for dz in range(3):
        w2 = w2_ref[dz].astype(BF)
        w2t[dz] = nt(eye, w2).astype(BF)
        low, high = nn(w2, to_low), nn(w2, to_high)
        tap = lambda half, dy, dx: half[(dy * 3 + dx) * 32:(dy * 3 + dx) * 32 + 32]
        at = dz * 128
        lmat[at:at + 32, 0:128] = tap(low, 1, 1).astype(BF)
        lmat[at + 32:at + 64, 0:128] = (tap(low, 1, 2) + tap(high, 1, 0)).astype(BF)
        lmat[at + 64:at + 96, 0:128] = tap(low, 2, 1).astype(BF)
        lmat[at + 96:at + 128, 0:128] = (tap(low, 2, 2) + tap(high, 2, 0)).astype(BF)
        lmat[at + 64:at + 96, 128:256] = tap(low, 0, 1).astype(BF)
        lmat[at + 96:at + 128, 128:256] = (tap(low, 0, 2) + tap(high, 0, 0)).astype(BF)
    moves[3].wait()
    repack(v_ref, 0, 4, sel, stage, d_ref, 0)
    moves[4].wait()
    repack(v_ref, 4, 4, sel, stage, d_ref, 4)
    first_section(t1, [pair_rows((d_ref, 1 + dz), (d_ref, 3 + dz)) for dz in range(3)], [(h_ref, 0), (h_ref, 1)])
    first_section(t1, [pair_rows((d_ref, 5 + dz)) for dz in range(3)], [(h_ref, 2)])
    moves[5].wait()
    d2_ref[1024:1152] = jnp.zeros((128, LANES), BF)

    def put(y, delta, left):
        d2_ref[y * 128:y * 128 + 64] = delta
        d2_ref[y * 128 + 64:y * 128 + 128] = left
        edge_ref[y * 64:y * 64 + 64] = delta

    second_section(w2t, [(h_ref, 0), (h_ref, 1), (h_ref, 2)], cot_ref, 1, rows_c, rows_a, put)
    act_ref[...] = rows_a[...].astype(BF).reshape(64, 8, LANES)


def slopes(ref, z, m):
    parts = [jnp.where(ref[z, (2 * m + i + 1) * 96 + 32:(2 * m + i + 1) * 96 + 96].astype(F32) > 0, 1.0, SLOPE) for i in range(2)]
    return jnp.concatenate(parts, axis=0)


def inner_kernel(share, packed, vh_ref, cot_ref, sel, t1, w2t, lmat, d_ref, h_ref, d2n, upper_ref,
                 act_ref, out_ref, g1_ref, grad_ref, dl_ref, hl_ref, stage, g2_ref, d2_ref, d1, rows_c, rows_a):
    clear(stage)
    repack(vh_ref, 0, 3, sel, stage, dl_ref, 0)
    first_section(t1, [pair_rows((dl_ref, 0), (dl_ref, 2)), pair_rows((dl_ref, 1), (d_ref, 0)), pair_rows((dl_ref, 2), (d_ref, 1))],
                  [(hl_ref, 0), (hl_ref, 1)])
    d2_ref[1024:1152] = jnp.zeros((128, LANES), BF)

    def put(y, delta, left):
        d2_ref[y * 128:y * 128 + 64] = delta
        d2_ref[y * 128 + 64:y * 128 + 128] = left

    second_section(w2t, [(hl_ref, 0), (hl_ref, 1), (h_ref, 0)], cot_ref, 0, rows_c, rows_a, put)
    act_ref[:, 0] = rows_a[...].astype(BF).reshape(64, 8, LANES)
    act_ref[:, 1] = upper_ref[...]
    lower = [(hl_ref, 0), (hl_ref, 1), (h_ref, 0)]
    for dz in range(3):
        acc = jnp.zeros((288, 64), F32)
        ref, z = lower[dz]
        for y in range(8):
            a = beside(ref[z, y * 192:y * 192 + 288], h_ref[dz, y * 192:y * 192 + 288])
            b = beside(d2_ref[y * 128:y * 128 + 64], d2n[y * 128:y * 128 + 64])
            acc += nt(a, b)
        g2_ref[dz * 288:dz * 288 + 288, 0:64] = acc
    g2_ref[864:872] = jnp.zeros((8, LANES), F32)
    if packed:
        count = share // 64
        low = lax.broadcasted_iota(jnp.int32, (14, LANES), 1) < 64
        for k in range(32):
            even = g2_ref[pl.ds(count * k, 14, stride=2), :]
            odd = g2_ref[pl.ds(count * k + 1, 14, stride=2), :]
            out_ref[k * 16:k * 16 + 14] = jnp.where(low, even, pltpu.roll(odd, 64, 1))
    else:
        out_ref[...] = g2_ref[...]
    for m in range(8):
        rows = slice(m * 128, m * 128 + 128)
        r = nn(lmat[...], beside(d2_ref[m * 128:m * 128 + 256], d2n[m * 128:m * 128 + 256]))
        r0, r1 = r[:, 0:LANES], r[:, LANES:2 * LANES]
        grad_ref[rows] = r0[0:128]
        d1[0, rows] = (r0[128:256] * slopes(hl_ref, 1, m)).astype(BF)
        d1[1, rows] = ((r0[256:384] + r1[0:128]) * slopes(h_ref, 0, m)).astype(BF)
        d1[2, rows] = (r1[128:256] * slopes(h_ref, 1, m)).astype(BF)
    lower = [(dl_ref, 2), (d_ref, 0), (d_ref, 1)]
    for dz in range(3):
        acc = jnp.zeros((128, REACH), F32)
        two, one = pair_rows(lower[dz], (d_ref, 1 + dz)), pair_rows((d_ref, 3 + dz))
        for m in range(8):
            rows = slice(m * 128, m * 128 + 128)
            acc += nt(beside(d1[0, rows], d1[1, rows]), two(m))
            acc += nt(d1[2, rows], one(m))
        g1_ref[dz] = acc

    @pl.when(lax.axis_index("space") == lax.axis_size("space") - 1)
    def _():
        for m in range(8):
            rows = slice(m * 128, m * 128 + 128)
            d1[0, rows] = (nn(lmat[256:384], d2n[m * 128:m * 128 + 256]) * slopes(h_ref, 2, m)).astype(BF)
        for dz in range(3):
            acc = g1_ref[dz]
            one = pair_rows((d_ref, 5 + dz))
            for m in range(8):
                acc += nt(d1[0, m * 128:m * 128 + 128], one(m))
            g1_ref[dz] = acc


def edge_kernel(packed, under_ref, lmat, dl_ref, hl_ref, g1_ref, grad_ref, *rest):
    pay_ref, out_ref, d2h, d1, lines = rest if packed else (None,) + rest
    lane = lax.broadcasted_iota(jnp.int32, (64, LANES), 1)
    d2h[1024:1152] = jnp.zeros((128, LANES), BF)
    for y in range(8):
        low = under_ref[y * 64:y * 64 + 64]
        left = jnp.where(lane == LANES - 1, 0.0, pltpu.roll(low.astype(F32), LANES - 1, 1))
        d2h[y * 128:y * 128 + 64] = low
        d2h[y * 128 + 64:y * 128 + 128] = left.astype(BF)
    for m in range(8):
        rows = slice(m * 128, m * 128 + 128)
        grad = grad_ref[rows] + nn(lmat[256:384], d2h[m * 128:m * 128 + 256])
        d1[rows] = (grad * slopes(hl_ref, 0, m)).astype(BF)
    lane = lax.broadcasted_iota(jnp.int32, (32, LANES), 1)
    total = jnp.zeros((32, LANES), F32)
    for dz in range(3):
        acc = g1_ref[dz]
        rows_of = pair_rows((dl_ref, dz))
        for m in range(8):
            acc += nt(d1[m * 128:m * 128 + 128], rows_of(m))
        wide = jnp.concatenate([acc, jnp.zeros((128, LANES - REACH), F32)], axis=1)
        part = jnp.zeros((32, LANES), F32)
        for i in range(2):
            for p in range(2):
                block = wide[(2 * i + p) * 32:(2 * i + p) * 32 + 32]
                shift = -(2 * i * SLOTS + 8 * p) % LANES
                part += block if shift == 0 else pltpu.roll(block, shift, 1)
        for dy in range(3):
            to = (dz * 3 + dy) * 12
            shift = (to - dy * SLOTS) % LANES
            total = jnp.where((lane >= to) & (lane < to + 12), part if shift == 0 else pltpu.roll(part, shift, 1), total)
    if not packed:
        out_ref[...] = total
        return
    lines[...] = pay_ref[...]
    lines[pl.ds(14, 32, stride=16), :] = total
    lines[pl.ds(15, 32, stride=16), :] = total - total.astype(BF).astype(F32)
    out_ref[...] = lines[...].astype(BF).reshape(32, 16, LANES)


def spread_kernel(count, full_ref, old_ref, kernel_ref, first_ref, lines):
    columns = []
    for k in range(32):
        x = full_ref[k].astype(F32)
        lines[pl.ds(count * k, 14, stride=2), :] = x[0:14]
        lines[pl.ds(count * k + 1, 13, stride=2), :] = pltpu.roll(x, 64, 1)[0:13]
        columns.append(x[14:15] + x[15:16])
    kernel_ref[...] = old_ref[...] - lines[0:864, 0:64]
    turned = jnp.concatenate(columns + [jnp.zeros((96, LANES), F32)], axis=0).T
    for j in range(27):
        first_ref[j] = turned[j * 4:j * 4 + 4, 0:32]


VMEM = pl.BlockSpec(memory_space=pltpu.VMEM)
HBM = pl.BlockSpec(memory_space=pltpu.HBM)
DMA = pltpu.SemaphoreType.DMA


def call(kernel, outs, scratch, args, at=VMEM):
    return pl.pallas_call(
        kernel,
        out_shape=[pltpu.VMEM(s, t) if stays else jax.ShapeDtypeStruct(s, t) for s, t, stays in outs],
        in_specs=[at] * len(args),
        out_specs=[VMEM] * len(outs),
        scratch_shapes=[DMA(s) if t is DMA else pltpu.VMEM(s, t) for s, t in scratch],
        compiler_params=pltpu.CompilerParams(vmem_limit_bytes=32 * 1024 * 1024),
    )(*args)


def stay(*arrays):
    return [pltpu.with_memory_space_constraint(a, pltpu.VMEM) for a in arrays]


def stay_out(arrays):
    return [pltpu.with_memory_space_constraint(a, pltpu.HBM) for a in arrays]


def gather(values, count):
    wide = jnp.broadcast_to(values[None], (count,) + values.shape)
    return lax.all_to_all(wide, AXES, 0, 0, tiled=True)


def shards(volumes, first_kernel, second_kernel, cotangent, first_moment, second_moment):
    count = lax.axis_size(AXES)
    share = first_moment.shape[0]
    packed = count == 32 and share == 1728
    below = along(volumes[0, :, -3:], "space", 1)
    deep = lambda n: ((n, DEEP, LANES), BF, True)
    hidden = lambda n: ((n, 1632, LANES), BF, True)
    plane = ((64, 8, LANES), BF, True)
    spread = ((1152, LANES), BF)
    flat = ((512, LANES), F32)
    sel, t1, w2t, lmat, d, h, cot, d2, edge, upper = call(
        own_kernel,
        [((512, 512), BF, True), ((3, 128, REACH), BF, True), ((3, 64, 288), BF, True), ((384, 256), BF, True), deep(8), hidden(3),
         ((64, 2, 8, LANES), BF, True), spread + (True,), ((512, LANES), BF, False), plane],
        [((4, DEEP, LANES), F32), flat, flat, ((3, 40, 32), F32),
         ((4, 8, 32, 512), BF), ((27, 4, 32), BF), ((36, 512), BF), ((3, 288, 64), F32), ((6,), DMA)],
        stay_out((volumes[0], first_kernel.reshape(27, 4, 32), jnp.asarray(spread_taps(), BF), second_kernel.reshape(3, 288, 64), cotangent[0])), HBM,
    )
    cot, sel, t1, w2t, lmat, d, h, d2, upper = stay(cot, sel, t1, w2t, lmat, d, h, d2, upper)
    under = along(edge, "space", 1)
    act, g2, g1, grad, dl, hl = call(
        functools.partial(inner_kernel, share, packed),
        [((64, 2, 8, LANES), BF, False), ((512, LANES) if packed else (872, LANES), F32, packed), ((3, 128, REACH), F32, True),
         ((1024, LANES), F32, True), deep(3), hidden(2)],
        [((3, DEEP, LANES), F32), ((872, LANES), F32), spread, ((3, 1024, LANES), BF), flat, flat],
        [below, cot, sel, t1, w2t, lmat, d, h, d2, upper],
    )
    (out,) = call(
        functools.partial(edge_kernel, packed),
        [((32, 16, LANES), BF, False) if packed else ((32, LANES), F32, False)],
        [spread, ((1024, LANES), BF), flat],
        [under, lmat] + stay(dl, hl, g1, grad) + (stay(g2) if packed else []),
    )
    if packed:
        both = lax.all_to_all(out, AXES, 0, 0, tiled=True).astype(F32).sum(0)
        one = both[14] + both[15]
        both = both.reshape(-1)
    else:
        one = out[:, :108].T.reshape(-1)
        one = jnp.pad(one, (0, -one.shape[0] % count)).reshape(count, -1)
        both = jnp.concatenate([g2[:864, :64].reshape(count, share), one], axis=1)
        both = lax.all_to_all(both, AXES, 0, 0, tiled=True).sum(0)
    grad_share = both[:share]
    new_first = BETA_FIRST * first_moment + (1.0 - BETA_FIRST) * grad_share
    new_second = BETA_SECOND * second_moment + (1.0 - BETA_SECOND) * grad_share * grad_share
    change = LEARN_RATE * new_first / (jnp.sqrt(new_second) + EPSILON)
    if packed:
        tail = jnp.stack([one, one - lax.reduce_precision(one, 8, 7)])
        send = jnp.concatenate([jnp.pad(change, (0, 64)).reshape(14, LANES), tail]).astype(BF)
        full = gather(send, count)
        new_kernel, first_gradient = call(
            functools.partial(spread_kernel, share // 64),
            [((864, 64), F32, False), ((27, 4, 32), F32, False)], [((880, LANES), F32)], (full, second_kernel.reshape(864, 64)))
    else:
        offset = lax.axis_index(AXES) * share
        kernel_share = lax.dynamic_slice_in_dim(second_kernel.reshape(-1), offset, share, 0)
        full = gather(jnp.concatenate([kernel_share - change, both[share:]]), count)
        new_kernel = full[:, :share]
        first_gradient = full[:, share:].reshape(-1)[:first_kernel.size]
    return (act[None], first_gradient.reshape(first_kernel.shape), new_kernel.reshape(second_kernel.shape), new_first, new_second)


def solution(mesh):
    field = P("dp", None, "space", None, None)
    flat = P(AXES)
    return jax.shard_map(
        shards, mesh=mesh, in_specs=(field, P(), P(), field, flat, flat),
        out_specs=(field, P(), P(), flat, flat), check_vma=False)
```

```python
import functools
import jax
import jax.numpy as jnp
import numpy as np
from jax import lax
from jax.experimental import pallas as pl
from jax.experimental.pallas import tpu as pltpu
from jax.sharding import PartitionSpec as P

SLOPE = 0.3
BETA_FIRST = 0.9
BETA_SECOND = 0.999
LEARN_RATE = 0.001
EPSILON = 1e-08
BF = jnp.bfloat16
F32 = jnp.float32
AXES = ("dp", "space")
LANES = 128
SLOTS = 20
REACH = 112
DEEP = 672


def along(value, axis, steps):
    count = lax.axis_size(axis)
    first, last = (max(0, -steps), min(count, count - steps))
    return lax.ppermute(value, axis, [(source, source + steps) for source in range(first, last)])


def leaky(values):
    return jnp.where(values > 0, values, SLOPE * values)


def nn(a, b):
    return lax.dot_general(a, b, (((1,), (0,)), ((), ())), preferred_element_type=F32)


def nt(a, b):
    return lax.dot_general(a, b, (((1,), (1,)), ((), ())), preferred_element_type=F32)


def tn(a, b):
    return lax.dot_general(a, b, (((0,), (0,)), ((), ())), preferred_element_type=F32)


def spread_taps():
    table = np.zeros((3, 3, 4, 2, 2, LANES), np.float32)
    for dy in range(3):
        for dx in range(3):
            for c in range(4):
                for row in range(2):
                    for p in range(2):
                        table[dy, dx, c, row, p, (2 * row + dy) * SLOTS + (2 * p + dx) * 4 + c] = 1
    return table.reshape(36, 512)


def repack(source, first, count, sel, stage, out, to):
    x = jnp.concatenate([source[:, first + i].reshape(4 * 32, 512) for i in range(count)], axis=0)
    lane = lax.broadcasted_iota(jnp.int32, (32, LANES), 1)
    for r0 in range(0, 4, 2):
        parts = nn(x, sel[:, r0 * LANES:(r0 + 2) * LANES])
        for r in range(r0, r0 + 2):
            part = parts[:, (r - r0) * LANES:(r - r0 + 1) * LANES]
            for i in range(count):
                for c in range(4):
                    block = part[i * 128 + c * 32:i * 128 + c * 32 + 32]
                    stage[i, pl.ds(SLOTS + (r + 1) * 4 + c, 32, stride=SLOTS), :] = block
                    if r == 3:
                        moved = jnp.where(lane == 0, 0.0, pltpu.roll(block, 1, 1))
                        stage[i, pl.ds(SLOTS + c, 32, stride=SLOTS), :] = moved
    for i in range(count):
        out[to + i] = stage[i].astype(BF)


def clear(stage):
    for i in range(stage.shape[0]):
        stage[i, 0:24] = jnp.zeros((24, LANES), F32)
        stage[i, 656:DEEP] = jnp.zeros((DEEP - 656, LANES), F32)


def first_section(t1, planes, outs):
    lane = lax.broadcasted_iota(jnp.int32, (32, LANES), 1)
    for ref, z in outs:
        ref[z, 0:96] = jnp.zeros((96, LANES), BF)
    for m in range(8):
        acc = nn(t1[0], planes[0](m))
        acc += nn(t1[1], planes[1](m))
        acc += nn(t1[2], planes[2](m))
        both = leaky(acc)
        for k, (ref, z) in enumerate(outs):
            hid = both[:, k * LANES:(k + 1) * LANES]
            for i in range(2):
                at = (2 * m + i + 1) * 96
                odd = hid[i * 64 + 32:i * 64 + 64]
                ref[z, at:at + 32] = jnp.where(lane == 0, 0.0, pltpu.roll(odd, 1, 1)).astype(BF)
                ref[z, at + 32:at + 96] = hid[i * 64:i * 64 + 64].astype(BF)


def beside(*parts):
    return parts[0] if len(parts) == 1 else jnp.concatenate(parts, axis=1)


def pair_rows(*places):
    return lambda m: beside(*[ref[z, m * 4 * SLOTS:m * 4 * SLOTS + REACH] for ref, z in places])


def second_section(w2t, planes, cot_ref, z, rows_c, rows_a, put):
    lane = lax.broadcasted_iota(jnp.int32, (64, LANES), 1)
    rows_c[...] = cot_ref[:, z].astype(F32).reshape(512, LANES)
    for y in range(8):
        acc = nn(w2t[0], planes[0][0][planes[0][1], y * 192:y * 192 + 288])
        acc += nn(w2t[1], planes[1][0][planes[1][1], y * 192:y * 192 + 288])
        acc += nn(w2t[2], planes[2][0][planes[2][1], y * 192:y * 192 + 288])
        rows_a[pl.ds(y, 64, stride=8), :] = leaky(acc)
        delta = rows_c[pl.ds(y, 64, stride=8), :] * jnp.where(acc > 0, 1.0, SLOPE)
        left = jnp.where(lane == LANES - 1, 0.0, pltpu.roll(delta, LANES - 1, 1))
        put(y, delta.astype(BF), left.astype(BF))


def own_kernel(v_hbm, w1_hbm, e_hbm, w2_hbm, cot_hbm, sel, t1, w2t, lmat, d_ref, h_ref, cot_ref, d2_ref, edge_ref, act_ref,
               stage, rows_c, rows_a, w1s, v_ref, w1_ref, e_ref, w2_ref, sems):
    moves = [pltpu.make_async_copy(source, target, sems.at[i]) for i, (source, target) in enumerate((
        (w1_hbm, w1_ref), (e_hbm, e_ref), (w2_hbm, w2_ref),
        (v_hbm.at[:, 0:4], v_ref.at[:, 0:4]), (v_hbm.at[:, 4:8], v_ref.at[:, 4:8]), (cot_hbm, cot_ref)))]
    for move in moves:
        move.start()
    lane = lax.broadcasted_iota(jnp.int32, (512, LANES), 1)
    row = lax.broadcasted_iota(jnp.int32, (512, LANES), 0)
    base = row - 4 * lane
    for r in range(4):
        sel[:, r * LANES:(r + 1) * LANES] = jnp.where(base == r, 1.0, 0.0).astype(BF)
    clear(stage)
    moves[0].wait()
    moves[1].wait()
    for j in range(27):
        w1s[j // 9, (j % 9) * 4:(j % 9) * 4 + 4, :] = w1_ref[j].astype(F32)
    for dz in range(3):
        taps = tn(w1s[dz, 0:36].astype(BF), e_ref[...]).astype(BF)
        for b in range(4):
            t1[dz, b * 32:(b + 1) * 32, :] = taps[:, b * LANES:b * LANES + REACH]
    eye = jnp.where(lax.broadcasted_iota(jnp.int32, (64, 64), 0) == lax.broadcasted_iota(jnp.int32, (64, 64), 1), 1.0, 0.0).astype(BF)
    step = lax.broadcasted_iota(jnp.int32, (64, LANES), 1) - lax.broadcasted_iota(jnp.int32, (64, LANES), 0)
    to_low = jnp.where(step == 0, 1.0, 0.0).astype(BF)
    to_high = jnp.where(step == 64, 1.0, 0.0).astype(BF)
    lmat[...] = jnp.zeros_like(lmat)
    moves[2].wait()
    for dz in range(3):
        w2 = w2_ref[dz].astype(BF)
        w2t[dz] = nt(eye, w2).astype(BF)
        low, high = nn(w2, to_low), nn(w2, to_high)
        tap = lambda half, dy, dx: half[(dy * 3 + dx) * 32:(dy * 3 + dx) * 32 + 32]
        at = dz * 128
        lmat[at:at + 32, 0:128] = tap(low, 1, 1).astype(BF)
        lmat[at + 32:at + 64, 0:128] = (tap(low, 1, 2) + tap(high, 1, 0)).astype(BF)
        lmat[at + 64:at + 96, 0:128] = tap(low, 2, 1).astype(BF)
        lmat[at + 96:at + 128, 0:128] = (tap(low, 2, 2) + tap(high, 2, 0)).astype(BF)
        lmat[at + 64:at + 96, 128:256] = tap(low, 0, 1).astype(BF)
        lmat[at + 96:at + 128, 128:256] = (tap(low, 0, 2) + tap(high, 0, 0)).astype(BF)
    moves[3].wait()
    repack(v_ref, 0, 4, sel, stage, d_ref, 0)
    moves[4].wait()
    repack(v_ref, 4, 4, sel, stage, d_ref, 4)
    first_section(t1, [pair_rows((d_ref, 1 + dz), (d_ref, 3 + dz)) for dz in range(3)], [(h_ref, 0), (h_ref, 1)])
    first_section(t1, [pair_rows((d_ref, 5 + dz)) for dz in range(3)], [(h_ref, 2)])
    moves[5].wait()
    d2_ref[1024:1152] = jnp.zeros((128, LANES), BF)

    def put(y, delta, left):
        d2_ref[y * 128:y * 128 + 64] = delta
        d2_ref[y * 128 + 64:y * 128 + 128] = left
        edge_ref[y * 64:y * 64 + 64] = delta

    second_section(w2t, [(h_ref, 0), (h_ref, 1), (h_ref, 2)], cot_ref, 1, rows_c, rows_a, put)
    act_ref[...] = rows_a[...].astype(BF).reshape(64, 8, LANES)


def slopes(ref, z, m):
    parts = [jnp.where(ref[z, (2 * m + i + 1) * 96 + 32:(2 * m + i + 1) * 96 + 96].astype(F32) > 0, 1.0, SLOPE) for i in range(2)]
    return jnp.concatenate(parts, axis=0)


def inner_kernel(share, packed, vh_ref, cot_ref, sel, t1, w2t, lmat, d_ref, h_ref, d2n, upper_ref,
                 act_ref, out_ref, g1_ref, grad_ref, dl_ref, hl_ref, stage, g2_ref, d2_ref, d1, rows_c, rows_a):
    clear(stage)
    repack(vh_ref, 0, 3, sel, stage, dl_ref, 0)
    first_section(t1, [pair_rows((dl_ref, 0), (dl_ref, 2)), pair_rows((dl_ref, 1), (d_ref, 0)), pair_rows((dl_ref, 2), (d_ref, 1))],
                  [(hl_ref, 0), (hl_ref, 1)])
    d2_ref[1024:1152] = jnp.zeros((128, LANES), BF)

    def put(y, delta, left):
        d2_ref[y * 128:y * 128 + 64] = delta
        d2_ref[y * 128 + 64:y * 128 + 128] = left

    second_section(w2t, [(hl_ref, 0), (hl_ref, 1), (h_ref, 0)], cot_ref, 0, rows_c, rows_a, put)
    act_ref[:, 0] = rows_a[...].astype(BF).reshape(64, 8, LANES)
    act_ref[:, 1] = upper_ref[...]
    lower = [(hl_ref, 0), (hl_ref, 1), (h_ref, 0)]
    for dz in range(3):
        acc = jnp.zeros((288, 64), F32)
        ref, z = lower[dz]
        for y in range(8):
            a = beside(ref[z, y * 192:y * 192 + 288], h_ref[dz, y * 192:y * 192 + 288])
            b = beside(d2_ref[y * 128:y * 128 + 64], d2n[y * 128:y * 128 + 64])
            acc += nt(a, b)
        g2_ref[dz * 288:dz * 288 + 288, 0:64] = acc
    g2_ref[864:872] = jnp.zeros((8, LANES), F32)
    if packed:
        count = share // 64
        low = lax.broadcasted_iota(jnp.int32, (14, LANES), 1) < 64
        for k in range(32):
            even = g2_ref[pl.ds(count * k, 14, stride=2), :]
            odd = g2_ref[pl.ds(count * k + 1, 14, stride=2), :]
            out_ref[k * 16:k * 16 + 14] = jnp.where(low, even, pltpu.roll(odd, 64, 1))
    else:
        out_ref[...] = g2_ref[...]
    for m in range(8):
        rows = slice(m * 128, m * 128 + 128)
        r = nn(lmat[...], beside(d2_ref[m * 128:m * 128 + 256], d2n[m * 128:m * 128 + 256]))
        r0, r1 = r[:, 0:LANES], r[:, LANES:2 * LANES]
        grad_ref[rows] = r0[0:128]
        d1[0, rows] = (r0[128:256] * slopes(hl_ref, 1, m)).astype(BF)
        d1[1, rows] = ((r0[256:384] + r1[0:128]) * slopes(h_ref, 0, m)).astype(BF)
        d1[2, rows] = (r1[128:256] * slopes(h_ref, 1, m)).astype(BF)
    lower = [(dl_ref, 2), (d_ref, 0), (d_ref, 1)]
    for dz in range(3):
        acc = jnp.zeros((128, REACH), F32)
        two, one = pair_rows(lower[dz], (d_ref, 1 + dz)), pair_rows((d_ref, 3 + dz))
        for m in range(8):
            rows = slice(m * 128, m * 128 + 128)
            acc += nt(beside(d1[0, rows], d1[1, rows]), two(m))
            acc += nt(d1[2, rows], one(m))
        g1_ref[dz] = acc

    @pl.when(lax.axis_index("space") == lax.axis_size("space") - 1)
    def _():
        for m in range(8):
            rows = slice(m * 128, m * 128 + 128)
            d1[0, rows] = (nn(lmat[256:384], d2n[m * 128:m * 128 + 256]) * slopes(h_ref, 2, m)).astype(BF)
        for dz in range(3):
            acc = g1_ref[dz]
            one = pair_rows((d_ref, 5 + dz))
            for m in range(8):
                acc += nt(d1[0, m * 128:m * 128 + 128], one(m))
            g1_ref[dz] = acc


def edge_kernel(packed, under_ref, lmat, dl_ref, hl_ref, g1_ref, grad_ref, *rest):
    pay_ref, out_ref, d2h, d1, lines = rest if packed else (None,) + rest
    lane = lax.broadcasted_iota(jnp.int32, (64, LANES), 1)
    d2h[1024:1152] = jnp.zeros((128, LANES), BF)
    for y in range(8):
        low = under_ref[y * 64:y * 64 + 64]
        left = jnp.where(lane == LANES - 1, 0.0, pltpu.roll(low.astype(F32), LANES - 1, 1))
        d2h[y * 128:y * 128 + 64] = low
        d2h[y * 128 + 64:y * 128 + 128] = left.astype(BF)
    for m in range(8):
        if m % 2 == 0:
            more = nn(lmat[256:384], beside(d2h[m * 128:m * 128 + 256], d2h[m * 128 + 128:m * 128 + 384]))
        rows = slice(m * 128, m * 128 + 128)
        grad = grad_ref[rows] + more[:, (m % 2) * LANES:(m % 2 + 1) * LANES]
        d1[rows] = (grad * slopes(hl_ref, 0, m)).astype(BF)
    lane = lax.broadcasted_iota(jnp.int32, (32, LANES), 1)
    total = jnp.zeros((32, LANES), F32)
    for dz in range(3):
        acc = g1_ref[dz]
        rows_of = pair_rows((dl_ref, dz))
        acc += nt(beside(*[d1[m * 128:m * 128 + 128] for m in range(8)]), beside(*[rows_of(m) for m in range(8)]))
        wide = jnp.concatenate([acc, jnp.zeros((128, LANES - REACH), F32)], axis=1)
        part = jnp.zeros((32, LANES), F32)
        for i in range(2):
            for p in range(2):
                block = wide[(2 * i + p) * 32:(2 * i + p) * 32 + 32]
                shift = -(2 * i * SLOTS + 8 * p) % LANES
                part += block if shift == 0 else pltpu.roll(block, shift, 1)
        for dy in range(3):
            to = (dz * 3 + dy) * 12
            shift = (to - dy * SLOTS) % LANES
            total = jnp.where((lane >= to) & (lane < to + 12), part if shift == 0 else pltpu.roll(part, shift, 1), total)
    if not packed:
        out_ref[...] = total
        return
    lines[...] = pay_ref[...]
    lines[pl.ds(14, 32, stride=16), :] = total
    lines[pl.ds(15, 32, stride=16), :] = total - total.astype(BF).astype(F32)
    out_ref[...] = lines[...].astype(BF).reshape(32, 16, LANES)


def spread_kernel(count, full_ref, old_ref, kernel_ref, first_ref, lines):
    columns = []
    for k in range(32):
        x = full_ref[k].astype(F32)
        lines[pl.ds(count * k, 14, stride=2), :] = x[0:14]
        lines[pl.ds(count * k + 1, 13, stride=2), :] = pltpu.roll(x, 64, 1)[0:13]
        columns.append(x[14:15] + x[15:16])
    kernel_ref[...] = old_ref[...] - lines[0:864, 0:64]
    turned = jnp.concatenate(columns + [jnp.zeros((96, LANES), F32)], axis=0).T
    for j in range(27):
        first_ref[j] = turned[j * 4:j * 4 + 4, 0:32]


VMEM = pl.BlockSpec(memory_space=pltpu.VMEM)
HBM = pl.BlockSpec(memory_space=pltpu.HBM)
DMA = pltpu.SemaphoreType.DMA


def call(kernel, outs, scratch, args, at=VMEM):
    return pl.pallas_call(
        kernel,
        out_shape=[pltpu.VMEM(s, t) if stays else jax.ShapeDtypeStruct(s, t) for s, t, stays in outs],
        in_specs=[at] * len(args),
        out_specs=[VMEM] * len(outs),
        scratch_shapes=[DMA(s) if t is DMA else pltpu.VMEM(s, t) for s, t in scratch],
        compiler_params=pltpu.CompilerParams(vmem_limit_bytes=32 * 1024 * 1024),
    )(*args)


def stay(*arrays):
    return [pltpu.with_memory_space_constraint(a, pltpu.VMEM) for a in arrays]


def stay_out(arrays):
    return [pltpu.with_memory_space_constraint(a, pltpu.HBM) for a in arrays]


def gather(values, count):
    wide = jnp.broadcast_to(values[None], (count,) + values.shape)
    return lax.all_to_all(wide, AXES, 0, 0, tiled=True)


def shards(volumes, first_kernel, second_kernel, cotangent, first_moment, second_moment):
    count = lax.axis_size(AXES)
    share = first_moment.shape[0]
    packed = count == 32 and share == 1728
    below = along(volumes[0, :, -3:], "space", 1)
    deep = lambda n: ((n, DEEP, LANES), BF, True)
    hidden = lambda n: ((n, 1632, LANES), BF, True)
    plane = ((64, 8, LANES), BF, True)
    spread = ((1152, LANES), BF)
    flat = ((512, LANES), F32)
    sel, t1, w2t, lmat, d, h, cot, d2, edge, upper = call(
        own_kernel,
        [((512, 512), BF, True), ((3, 128, REACH), BF, True), ((3, 64, 288), BF, True), ((384, 256), BF, True), deep(8), hidden(3),
         ((64, 2, 8, LANES), BF, True), spread + (True,), ((512, LANES), BF, False), plane],
        [((4, DEEP, LANES), F32), flat, flat, ((3, 40, 32), F32),
         ((4, 8, 32, 512), BF), ((27, 4, 32), BF), ((36, 512), BF), ((3, 288, 64), F32), ((6,), DMA)],
        stay_out((volumes[0], first_kernel.reshape(27, 4, 32), jnp.asarray(spread_taps(), BF), second_kernel.reshape(3, 288, 64), cotangent[0])), HBM,
    )
    cot, sel, t1, w2t, lmat, d, h, d2, upper = stay(cot, sel, t1, w2t, lmat, d, h, d2, upper)
    under = along(edge, "space", 1)
    act, g2, g1, grad, dl, hl = call(
        functools.partial(inner_kernel, share, packed),
        [((64, 2, 8, LANES), BF, False), ((512, LANES) if packed else (872, LANES), F32, packed), ((3, 128, REACH), F32, True),
         ((1024, LANES), F32, True), deep(3), hidden(2)],
        [((3, DEEP, LANES), F32), ((872, LANES), F32), spread, ((3, 1024, LANES), BF), flat, flat],
        [below, cot, sel, t1, w2t, lmat, d, h, d2, upper],
    )
    (out,) = call(
        functools.partial(edge_kernel, packed),
        [((32, 16, LANES), BF, False) if packed else ((32, LANES), F32, False)],
        [spread, ((1024, LANES), BF), flat],
        [under, lmat] + stay(dl, hl, g1, grad) + (stay(g2) if packed else []),
    )
    if packed:
        both = lax.all_to_all(out, AXES, 0, 0, tiled=True).astype(F32).sum(0)
        one = both[14] + both[15]
        both = both.reshape(-1)
    else:
        one = out[:, :108].T.reshape(-1)
        one = jnp.pad(one, (0, -one.shape[0] % count)).reshape(count, -1)
        both = jnp.concatenate([g2[:864, :64].reshape(count, share), one], axis=1)
        both = lax.all_to_all(both, AXES, 0, 0, tiled=True).sum(0)
    grad_share = both[:share]
    new_first = BETA_FIRST * first_moment + (1.0 - BETA_FIRST) * grad_share
    new_second = BETA_SECOND * second_moment + (1.0 - BETA_SECOND) * grad_share * grad_share
    change = LEARN_RATE * new_first / (jnp.sqrt(new_second) + EPSILON)
    if packed:
        tail = jnp.stack([one, one - lax.reduce_precision(one, 8, 7)])
        send = jnp.concatenate([jnp.pad(change, (0, 64)).reshape(14, LANES), tail]).astype(BF)
        full = gather(send, count)
        new_kernel, first_gradient = call(
            functools.partial(spread_kernel, share // 64),
            [((864, 64), F32, False), ((27, 4, 32), F32, False)], [((880, LANES), F32)], (full, second_kernel.reshape(864, 64)))
    else:
        offset = lax.axis_index(AXES) * share
        kernel_share = lax.dynamic_slice_in_dim(second_kernel.reshape(-1), offset, share, 0)
        full = gather(jnp.concatenate([kernel_share - change, both[share:]]), count)
        new_kernel = full[:, :share]
        first_gradient = full[:, share:].reshape(-1)[:first_kernel.size]
    return (act[None], first_gradient.reshape(first_kernel.shape), new_kernel.reshape(second_kernel.shape), new_first, new_second)


def solution(mesh):
    field = P("dp", None, "space", None, None)
    flat = P(AXES)
    return jax.shard_map(
        shards, mesh=mesh, in_specs=(field, P(), P(), field, flat, flat),
        out_specs=(field, P(), P(), flat, flat), check_vma=False)
```

```python
import functools
import jax
import jax.numpy as jnp
import numpy as np
from jax import lax
from jax.experimental import pallas as pl
from jax.experimental.pallas import tpu as pltpu
from jax.sharding import PartitionSpec as P

SLOPE = 0.3
BETA_FIRST = 0.9
BETA_SECOND = 0.999
LEARN_RATE = 0.001
EPSILON = 1e-08
BF = jnp.bfloat16
F32 = jnp.float32
AXES = ("dp", "space")
LANES = 128
SLOTS = 20
REACH = 112
DEEP = 672


def along(value, axis, steps):
    count = lax.axis_size(axis)
    first, last = (max(0, -steps), min(count, count - steps))
    return lax.ppermute(value, axis, [(source, source + steps) for source in range(first, last)])


def leaky(values):
    return jnp.where(values > 0, values, SLOPE * values)


def nn(a, b):
    return lax.dot_general(a, b, (((1,), (0,)), ((), ())), preferred_element_type=F32)


def nt(a, b):
    return lax.dot_general(a, b, (((1,), (1,)), ((), ())), preferred_element_type=F32)


def tn(a, b):
    return lax.dot_general(a, b, (((0,), (0,)), ((), ())), preferred_element_type=F32)


def spread_taps():
    table = np.zeros((3, 3, 4, 2, 2, LANES), np.float32)
    for dy in range(3):
        for dx in range(3):
            for c in range(4):
                for row in range(2):
                    for p in range(2):
                        table[dy, dx, c, row, p, (2 * row + dy) * SLOTS + (2 * p + dx) * 4 + c] = 1
    return table.reshape(36, 512)


def repack(source, first, count, sel, stage, out, to):
    x = jnp.concatenate([source[:, first + i].reshape(4 * 32, 512) for i in range(count)], axis=0)
    lane = lax.broadcasted_iota(jnp.int32, (32, LANES), 1)
    for r0 in range(0, 4, 2):
        parts = nn(x, sel[:, r0 * LANES:(r0 + 2) * LANES])
        for r in range(r0, r0 + 2):
            part = parts[:, (r - r0) * LANES:(r - r0 + 1) * LANES]
            for i in range(count):
                for c in range(4):
                    block = part[i * 128 + c * 32:i * 128 + c * 32 + 32]
                    stage[i, pl.ds(SLOTS + (r + 1) * 4 + c, 32, stride=SLOTS), :] = block
                    if r == 3:
                        moved = jnp.where(lane == 0, 0.0, pltpu.roll(block, 1, 1))
                        stage[i, pl.ds(SLOTS + c, 32, stride=SLOTS), :] = moved
    for i in range(count):
        out[to + i] = stage[i].astype(BF)


def clear(stage):
    for i in range(stage.shape[0]):
        stage[i, 0:24] = jnp.zeros((24, LANES), F32)
        stage[i, 656:DEEP] = jnp.zeros((DEEP - 656, LANES), F32)


def first_section(t1, planes, outs):
    lane = lax.broadcasted_iota(jnp.int32, (32, LANES), 1)
    for ref, z in outs:
        ref[z, 0:96] = jnp.zeros((96, LANES), BF)
    for m in range(8):
        acc = nn(t1[0], planes[0](m))
        acc += nn(t1[1], planes[1](m))
        acc += nn(t1[2], planes[2](m))
        both = leaky(acc)
        for k, (ref, z) in enumerate(outs):
            hid = both[:, k * LANES:(k + 1) * LANES]
            for i in range(2):
                at = (2 * m + i + 1) * 96
                odd = hid[i * 64 + 32:i * 64 + 64]
                ref[z, at:at + 32] = jnp.where(lane == 0, 0.0, pltpu.roll(odd, 1, 1)).astype(BF)
                ref[z, at + 32:at + 96] = hid[i * 64:i * 64 + 64].astype(BF)


def beside(*parts):
    return parts[0] if len(parts) == 1 else jnp.concatenate(parts, axis=1)


def pair_rows(*places):
    return lambda m: beside(*[ref[z, m * 4 * SLOTS:m * 4 * SLOTS + REACH] for ref, z in places])


def second_section(w2t, planes, cot_ref, z, rows_c, rows_a, put):
    lane = lax.broadcasted_iota(jnp.int32, (64, LANES), 1)
    rows_c[...] = cot_ref[:, z].astype(F32).reshape(512, LANES)
    for y in range(8):
        if y % 2 == 0:
            both = sum(nn(w2t[dz], beside(*[ref[at, k * 192:k * 192 + 288] for k in (y, y + 1)])) for dz, (ref, at) in enumerate(planes))
        acc = both[:, (y % 2) * LANES:(y % 2 + 1) * LANES]
        rows_a[pl.ds(y, 64, stride=8), :] = leaky(acc)
        delta = rows_c[pl.ds(y, 64, stride=8), :] * jnp.where(acc > 0, 1.0, SLOPE)
        left = jnp.where(lane == LANES - 1, 0.0, pltpu.roll(delta, LANES - 1, 1))
        put(y, delta.astype(BF), left.astype(BF))


def own_kernel(v_hbm, w1_hbm, e_hbm, w2_hbm, cot_hbm, sel, t1, w2t, lmat, d_ref, h_ref, cot_ref, d2_ref, edge_ref, act_ref,
               stage, rows_c, rows_a, w1s, v_ref, w1_ref, e_ref, w2_ref, sems):
    moves = [pltpu.make_async_copy(source, target, sems.at[i]) for i, (source, target) in enumerate((
        (w1_hbm, w1_ref), (e_hbm, e_ref), (w2_hbm, w2_ref),
        (v_hbm.at[:, 0:4], v_ref.at[:, 0:4]), (v_hbm.at[:, 4:8], v_ref.at[:, 4:8]), (cot_hbm, cot_ref)))]
    for move in moves:
        move.start()
    lane = lax.broadcasted_iota(jnp.int32, (512, LANES), 1)
    row = lax.broadcasted_iota(jnp.int32, (512, LANES), 0)
    base = row - 4 * lane
    for r in range(4):
        sel[:, r * LANES:(r + 1) * LANES] = jnp.where(base == r, 1.0, 0.0).astype(BF)
    clear(stage)
    moves[0].wait()
    moves[1].wait()
    for j in range(27):
        w1s[j // 9, (j % 9) * 4:(j % 9) * 4 + 4, :] = w1_ref[j].astype(F32)
    for dz in range(3):
        taps = tn(w1s[dz, 0:36].astype(BF), e_ref[...]).astype(BF)
        for b in range(4):
            t1[dz, b * 32:(b + 1) * 32, :] = taps[:, b * LANES:b * LANES + REACH]
    eye = jnp.where(lax.broadcasted_iota(jnp.int32, (64, 64), 0) == lax.broadcasted_iota(jnp.int32, (64, 64), 1), 1.0, 0.0).astype(BF)
    step = lax.broadcasted_iota(jnp.int32, (64, LANES), 1) - lax.broadcasted_iota(jnp.int32, (64, LANES), 0)
    to_low = jnp.where(step == 0, 1.0, 0.0).astype(BF)
    to_high = jnp.where(step == 64, 1.0, 0.0).astype(BF)
    lmat[...] = jnp.zeros_like(lmat)
    moves[2].wait()
    for dz in range(3):
        w2 = w2_ref[dz].astype(BF)
        w2t[dz] = nt(eye, w2).astype(BF)
        low, high = nn(w2, to_low), nn(w2, to_high)
        tap = lambda half, dy, dx: half[(dy * 3 + dx) * 32:(dy * 3 + dx) * 32 + 32]
        at = dz * 128
        lmat[at:at + 32, 0:128] = tap(low, 1, 1).astype(BF)
        lmat[at + 32:at + 64, 0:128] = (tap(low, 1, 2) + tap(high, 1, 0)).astype(BF)
        lmat[at + 64:at + 96, 0:128] = tap(low, 2, 1).astype(BF)
        lmat[at + 96:at + 128, 0:128] = (tap(low, 2, 2) + tap(high, 2, 0)).astype(BF)
        lmat[at + 64:at + 96, 128:256] = tap(low, 0, 1).astype(BF)
        lmat[at + 96:at + 128, 128:256] = (tap(low, 0, 2) + tap(high, 0, 0)).astype(BF)
    moves[3].wait()
    repack(v_ref, 0, 4, sel, stage, d_ref, 0)
    moves[4].wait()
    repack(v_ref, 4, 4, sel, stage, d_ref, 4)
    first_section(t1, [pair_rows((d_ref, 1 + dz), (d_ref, 3 + dz)) for dz in range(3)], [(h_ref, 0), (h_ref, 1)])
    first_section(t1, [pair_rows((d_ref, 5 + dz)) for dz in range(3)], [(h_ref, 2)])
    moves[5].wait()
    d2_ref[1024:1152] = jnp.zeros((128, LANES), BF)

    def put(y, delta, left):
        d2_ref[y * 128:y * 128 + 64] = delta
        d2_ref[y * 128 + 64:y * 128 + 128] = left
        edge_ref[y * 64:y * 64 + 64] = delta

    second_section(w2t, [(h_ref, 0), (h_ref, 1), (h_ref, 2)], cot_ref, 1, rows_c, rows_a, put)
    act_ref[...] = rows_a[...].astype(BF).reshape(64, 8, LANES)


def slopes(ref, z, m):
    parts = [jnp.where(ref[z, (2 * m + i + 1) * 96 + 32:(2 * m + i + 1) * 96 + 96].astype(F32) > 0, 1.0, SLOPE) for i in range(2)]
    return jnp.concatenate(parts, axis=0)


def inner_kernel(share, packed, vh_ref, cot_ref, sel, t1, w2t, lmat, d_ref, h_ref, d2n, upper_ref,
                 act_ref, out_ref, g1_ref, grad_ref, dl_ref, hl_ref, stage, g2_ref, d2_ref, d1, rows_c, rows_a):
    clear(stage)
    repack(vh_ref, 0, 3, sel, stage, dl_ref, 0)
    first_section(t1, [pair_rows((dl_ref, 0), (dl_ref, 2)), pair_rows((dl_ref, 1), (d_ref, 0)), pair_rows((dl_ref, 2), (d_ref, 1))],
                  [(hl_ref, 0), (hl_ref, 1)])
    d2_ref[1024:1152] = jnp.zeros((128, LANES), BF)

    def put(y, delta, left):
        d2_ref[y * 128:y * 128 + 64] = delta
        d2_ref[y * 128 + 64:y * 128 + 128] = left

    second_section(w2t, [(hl_ref, 0), (hl_ref, 1), (h_ref, 0)], cot_ref, 0, rows_c, rows_a, put)
    act_ref[:, 0] = rows_a[...].astype(BF).reshape(64, 8, LANES)
    act_ref[:, 1] = upper_ref[...]
    lower = [(hl_ref, 0), (hl_ref, 1), (h_ref, 0)]
    for dz in range(3):
        acc = jnp.zeros((288, 64), F32)
        ref, z = lower[dz]
        for y in range(8):
            a = beside(ref[z, y * 192:y * 192 + 288], h_ref[dz, y * 192:y * 192 + 288])
            b = beside(d2_ref[y * 128:y * 128 + 64], d2n[y * 128:y * 128 + 64])
            acc += nt(a, b)
        g2_ref[dz * 288:dz * 288 + 288, 0:64] = acc
    g2_ref[864:872] = jnp.zeros((8, LANES), F32)
    if packed:
        count = share // 64
        low = lax.broadcasted_iota(jnp.int32, (14, LANES), 1) < 64
        for k in range(32):
            even = g2_ref[pl.ds(count * k, 14, stride=2), :]
            odd = g2_ref[pl.ds(count * k + 1, 14, stride=2), :]
            out_ref[k * 16:k * 16 + 14] = jnp.where(low, even, pltpu.roll(odd, 64, 1))
    else:
        out_ref[...] = g2_ref[...]
    for m in range(8):
        rows = slice(m * 128, m * 128 + 128)
        r = nn(lmat[...], beside(d2_ref[m * 128:m * 128 + 256], d2n[m * 128:m * 128 + 256]))
        r0, r1 = r[:, 0:LANES], r[:, LANES:2 * LANES]
        grad_ref[rows] = r0[0:128]
        d1[0, rows] = (r0[128:256] * slopes(hl_ref, 1, m)).astype(BF)
        d1[1, rows] = ((r0[256:384] + r1[0:128]) * slopes(h_ref, 0, m)).astype(BF)
        d1[2, rows] = (r1[128:256] * slopes(h_ref, 1, m)).astype(BF)
    lower = [(dl_ref, 2), (d_ref, 0), (d_ref, 1)]
    for dz in range(3):
        acc = jnp.zeros((128, REACH), F32)
        two, one = pair_rows(lower[dz], (d_ref, 1 + dz)), pair_rows((d_ref, 3 + dz))
        for m in range(8):
            rows = slice(m * 128, m * 128 + 128)
            acc += nt(beside(d1[0, rows], d1[1, rows]), two(m))
            acc += nt(d1[2, rows], one(m))
        g1_ref[dz] = acc

    @pl.when(lax.axis_index("space") == lax.axis_size("space") - 1)
    def _():
        for m in range(8):
            rows = slice(m * 128, m * 128 + 128)
            d1[0, rows] = (nn(lmat[256:384], d2n[m * 128:m * 128 + 256]) * slopes(h_ref, 2, m)).astype(BF)
        for dz in range(3):
            acc = g1_ref[dz]
            one = pair_rows((d_ref, 5 + dz))
            for m in range(8):
                acc += nt(d1[0, m * 128:m * 128 + 128], one(m))
            g1_ref[dz] = acc


def edge_kernel(packed, under_ref, lmat, dl_ref, hl_ref, g1_ref, grad_ref, *rest):
    pay_ref, out_ref, d2h, d1, lines = rest if packed else (None,) + rest
    lane = lax.broadcasted_iota(jnp.int32, (64, LANES), 1)
    d2h[1024:1152] = jnp.zeros((128, LANES), BF)
    for y in range(8):
        low = under_ref[y * 64:y * 64 + 64]
        left = jnp.where(lane == LANES - 1, 0.0, pltpu.roll(low.astype(F32), LANES - 1, 1))
        d2h[y * 128:y * 128 + 64] = low
        d2h[y * 128 + 64:y * 128 + 128] = left.astype(BF)
    for m in range(8):
        if m % 2 == 0:
            more = nn(lmat[256:384], beside(d2h[m * 128:m * 128 + 256], d2h[m * 128 + 128:m * 128 + 384]))
        rows = slice(m * 128, m * 128 + 128)
        grad = grad_ref[rows] + more[:, (m % 2) * LANES:(m % 2 + 1) * LANES]
        d1[rows] = (grad * slopes(hl_ref, 0, m)).astype(BF)
    lane = lax.broadcasted_iota(jnp.int32, (32, LANES), 1)
    total = jnp.zeros((32, LANES), F32)
    for dz in range(3):
        acc = g1_ref[dz]
        rows_of = pair_rows((dl_ref, dz))
        acc += nt(beside(*[d1[m * 128:m * 128 + 128] for m in range(8)]), beside(*[rows_of(m) for m in range(8)]))
        wide = jnp.concatenate([acc, jnp.zeros((128, LANES - REACH), F32)], axis=1)
        part = jnp.zeros((32, LANES), F32)
        for i in range(2):
            for p in range(2):
                block = wide[(2 * i + p) * 32:(2 * i + p) * 32 + 32]
                shift = -(2 * i * SLOTS + 8 * p) % LANES
                part += block if shift == 0 else pltpu.roll(block, shift, 1)
        for dy in range(3):
            to = (dz * 3 + dy) * 12
            shift = (to - dy * SLOTS) % LANES
            total = jnp.where((lane >= to) & (lane < to + 12), part if shift == 0 else pltpu.roll(part, shift, 1), total)
    if not packed:
        out_ref[...] = total
        return
    lines[...] = pay_ref[...]
    lines[pl.ds(14, 32, stride=16), :] = total
    lines[pl.ds(15, 32, stride=16), :] = total - total.astype(BF).astype(F32)
    out_ref[...] = lines[...].astype(BF).reshape(32, 16, LANES)


def spread_kernel(count, full_ref, old_ref, kernel_ref, first_ref, lines):
    columns = []
    for k in range(32):
        x = full_ref[k].astype(F32)
        lines[pl.ds(count * k, 14, stride=2), :] = x[0:14]
        lines[pl.ds(count * k + 1, 13, stride=2), :] = pltpu.roll(x, 64, 1)[0:13]
        columns.append(x[14:15] + x[15:16])
    kernel_ref[...] = old_ref[...] - lines[0:864, 0:64]
    turned = jnp.concatenate(columns + [jnp.zeros((96, LANES), F32)], axis=0).T
    for j in range(27):
        first_ref[j] = turned[j * 4:j * 4 + 4, 0:32]


VMEM = pl.BlockSpec(memory_space=pltpu.VMEM)
HBM = pl.BlockSpec(memory_space=pltpu.HBM)
DMA = pltpu.SemaphoreType.DMA


def call(kernel, outs, scratch, args, at=VMEM):
    return pl.pallas_call(
        kernel,
        out_shape=[pltpu.VMEM(s, t) if stays else jax.ShapeDtypeStruct(s, t) for s, t, stays in outs],
        in_specs=[at] * len(args),
        out_specs=[VMEM] * len(outs),
        scratch_shapes=[DMA(s) if t is DMA else pltpu.VMEM(s, t) for s, t in scratch],
        compiler_params=pltpu.CompilerParams(vmem_limit_bytes=32 * 1024 * 1024),
    )(*args)


def stay(*arrays):
    return [pltpu.with_memory_space_constraint(a, pltpu.VMEM) for a in arrays]


def stay_out(arrays):
    return [pltpu.with_memory_space_constraint(a, pltpu.HBM) for a in arrays]


def gather(values, count):
    wide = jnp.broadcast_to(values[None], (count,) + values.shape)
    return lax.all_to_all(wide, AXES, 0, 0, tiled=True)


def shards(volumes, first_kernel, second_kernel, cotangent, first_moment, second_moment):
    count = lax.axis_size(AXES)
    share = first_moment.shape[0]
    packed = count == 32 and share == 1728
    below = along(volumes[0, :, -3:], "space", 1)
    deep = lambda n: ((n, DEEP, LANES), BF, True)
    hidden = lambda n: ((n, 1632, LANES), BF, True)
    plane = ((64, 8, LANES), BF, True)
    spread = ((1152, LANES), BF)
    flat = ((512, LANES), F32)
    sel, t1, w2t, lmat, d, h, cot, d2, edge, upper = call(
        own_kernel,
        [((512, 512), BF, True), ((3, 128, REACH), BF, True), ((3, 64, 288), BF, True), ((384, 256), BF, True), deep(8), hidden(3),
         ((64, 2, 8, LANES), BF, True), spread + (True,), ((512, LANES), BF, False), plane],
        [((4, DEEP, LANES), F32), flat, flat, ((3, 40, 32), F32),
         ((4, 8, 32, 512), BF), ((27, 4, 32), BF), ((36, 512), BF), ((3, 288, 64), F32), ((6,), DMA)],
        stay_out((volumes[0], first_kernel.reshape(27, 4, 32), jnp.asarray(spread_taps(), BF), second_kernel.reshape(3, 288, 64), cotangent[0])), HBM,
    )
    cot, sel, t1, w2t, lmat, d, h, d2, upper = stay(cot, sel, t1, w2t, lmat, d, h, d2, upper)
    under = along(edge, "space", 1)
    act, g2, g1, grad, dl, hl = call(
        functools.partial(inner_kernel, share, packed),
        [((64, 2, 8, LANES), BF, False), ((512, LANES) if packed else (872, LANES), F32, packed), ((3, 128, REACH), F32, True),
         ((1024, LANES), F32, True), deep(3), hidden(2)],
        [((3, DEEP, LANES), F32), ((872, LANES), F32), spread, ((3, 1024, LANES), BF), flat, flat],
        [below, cot, sel, t1, w2t, lmat, d, h, d2, upper],
    )
    (out,) = call(
        functools.partial(edge_kernel, packed),
        [((32, 16, LANES), BF, False) if packed else ((32, LANES), F32, False)],
        [spread, ((1024, LANES), BF), flat],
        [under, lmat] + stay(dl, hl, g1, grad) + (stay(g2) if packed else []),
    )
    if packed:
        both = lax.all_to_all(out, AXES, 0, 0, tiled=True).astype(F32).sum(0)
        one = both[14] + both[15]
        both = both.reshape(-1)
    else:
        one = out[:, :108].T.reshape(-1)
        one = jnp.pad(one, (0, -one.shape[0] % count)).reshape(count, -1)
        both = jnp.concatenate([g2[:864, :64].reshape(count, share), one], axis=1)
        both = lax.all_to_all(both, AXES, 0, 0, tiled=True).sum(0)
    grad_share = both[:share]
    new_first = BETA_FIRST * first_moment + (1.0 - BETA_FIRST) * grad_share
    new_second = BETA_SECOND * second_moment + (1.0 - BETA_SECOND) * grad_share * grad_share
    change = LEARN_RATE * new_first / (jnp.sqrt(new_second) + EPSILON)
    if packed:
        tail = jnp.stack([one, one - lax.reduce_precision(one, 8, 7)])
        send = jnp.concatenate([jnp.pad(change, (0, 64)).reshape(14, LANES), tail]).astype(BF)
        full = gather(send, count)
        new_kernel, first_gradient = call(
            functools.partial(spread_kernel, share // 64),
            [((864, 64), F32, False), ((27, 4, 32), F32, False)], [((880, LANES), F32)], (full, second_kernel.reshape(864, 64)))
    else:
        offset = lax.axis_index(AXES) * share
        kernel_share = lax.dynamic_slice_in_dim(second_kernel.reshape(-1), offset, share, 0)
        full = gather(jnp.concatenate([kernel_share - change, both[share:]]), count)
        new_kernel = full[:, :share]
        first_gradient = full[:, share:].reshape(-1)[:first_kernel.size]
    return (act[None], first_gradient.reshape(first_kernel.shape), new_kernel.reshape(second_kernel.shape), new_first, new_second)


def solution(mesh):
    field = P("dp", None, "space", None, None)
    flat = P(AXES)
    return jax.shard_map(
        shards, mesh=mesh, in_specs=(field, P(), P(), field, flat, flat),
        out_specs=(field, P(), P(), flat, flat), check_vma=False)
```
